32 devices in a mesh: seq: 8 (over z, y), vocab: 4 (over x, core).
Axes of the slice: x: 2, y: 2, z: 4, core: 2. Of those that a mesh axis runs over, the one named last changes fastest.
Arguments:
- q_noised: bfloat16 [1024, 4096], P('seq', 'vocab'), may hold values from -50 to 50
- key_clean: bfloat16 [1024, 1024], P('seq', 'vocab'), may hold values from -5 to 5
- value_clean: bfloat16 [1024, 1024], P('seq', 'vocab'), may hold values from -5 to 5
- key_noised: bfloat16 [1024, 1024], P('seq', 'vocab'), may hold values from -5 to 5
- value_noised: bfloat16 [1024, 1024], P('seq', 'vocab'), may hold values from -5 to 5
- out_weight: bfloat16 [4096, 4096], P('vocab'), may hold values from -0.09375 to 0.09375
- residual: bfloat16 [1024, 4096], P('seq'), may hold values from -52 to 52
- norm_gain: float32 [4096], replicated, may hold values from 0.5 to 1.5
- head_weight: bfloat16 [18944, 4096], P(('seq', 'vocab')), may hold values from -2 to 2
- targets: int32 [1024], replicated, may hold values from 0 to 18943
- mask_flags: int32 [1024], replicated, may hold values from 0 to 1, as said below
- levels: int32 [32], replicated, may hold values from 0 to 11, as said below
Outputs:
- token_loss: float32 [1024], P('seq')
The draws below stay inside these ranges and needn't reach their ends.
Inputs may be any that keep to these rules, and one draw needn't show every extreme that they name: `mask_flags`: within every block of 32 positions exactly levels + 1 flags are 1; the 128 positions of one index of seq hold at most 48 ones, and some index holds exactly 48 in every draw. `levels`: every block of some index of seq has level 11.
All inputs are finite; a program needn't handle non-finite values.
Results may differ from the reference program's by a relative error of at most 0.00077.
Values may be sent and summed in bfloat16 or wider, within the bound.
No kernel may reach another device: no remote copies, remote signals or barrier semaphores. Data moves between devices by JAX's collectives and lax.ppermute only.
A program may use at most 128 MiB of HBM per device.

```python
import math
import jax
import jax.numpy as jnp
import numpy as np
from jax import lax

D = 4096
HEADS = 32
KV_HEADS = 8
HEAD_DIM = 128
BLOCK = 32
LEVELS = 12
TOK_DEV = 128
KV_WIDTH = 1024
TOKENS = 1024
BLOCKS = 32
CAP = 48
VOCAB = 18944
N_SEQ = 8


def attention_pair(key):
    base = jax.random.fold_in(key, 21)
    first_key, second_key = jax.random.split(base, 2)
    kv_width = KV_HEADS * HEAD_DIM
    queries = jnp.clip(jax.random.normal(first_key, (TOKENS, D), jnp.float32), -5.0, 5.0)
    keys = jnp.clip(jax.random.normal(second_key, (TOKENS, kv_width), jnp.float32), -5.0, 5.0)
    return (queries, keys)


def vocab_pair(key):
    base = jax.random.fold_in(key, 33)
    first_key = jax.random.fold_in(base, 0)
    third_key = jax.random.fold_in(base, 2)
    rows = jnp.clip(jax.random.normal(first_key, (TOKENS, D), jnp.float32), -5.0, 5.0)
    weights = jnp.clip(jax.random.normal(third_key, (VOCAB, D), jnp.float32) * 0.047, -0.3, 0.3)
    return (rows, weights)


def mask_parts(key):
    base = jax.random.fold_in(key, 11)
    first_key, second_key, third_key = jax.random.split(base, 3)
    per_device = TOK_DEV // BLOCK
    device_count = BLOCKS // per_device
    level_draw = jax.random.randint(first_key, (BLOCKS,), 0, LEVELS)
    full_device = jax.random.randint(second_key, (), 0, device_count)
    device_of_block = jnp.arange(BLOCKS) // per_device
    level_draw = jnp.where(device_of_block == full_device, LEVELS - 1, level_draw).astype(jnp.int32)
    ranking = jax.random.randint(third_key, (BLOCKS, BLOCK), 0, 2 ** 20) * BLOCK + jnp.arange(BLOCK)[None, :]
    ranks = jnp.argsort(jnp.argsort(ranking, axis=1), axis=1)
    flags = (ranks < level_draw[:, None] + 1).astype(jnp.int32).reshape(TOKENS)
    return (flags, level_draw)


def draw_q_noised(key, part):
    return attention_pair(key)[0].astype(jnp.bfloat16)


def draw_key_clean(key, part):
    return attention_pair(key)[1].astype(jnp.bfloat16)


def draw_residual(key, part):
    return vocab_pair(key)[0].astype(jnp.bfloat16)


def draw_head_weight(key, part):
    return vocab_pair(key)[1].astype(jnp.bfloat16)


def draw_mask_flags(key, part):
    return mask_parts(key)[0]


def draw_levels(key, part):
    return mask_parts(key)[1]


def plant(result, rng, least, high):
    index_at = [jax.random.randint(jax.random.fold_in(rng, axis), (), 0, length) for axis, length in enumerate(result.shape)]
    main_axis = result.shape.index(max(result.shape))
    neighbour = index_at[:main_axis] + [(index_at[main_axis] + 1) % result.shape[main_axis]] + index_at[main_axis + 1:]
    return result.at[tuple(index_at)].set(least).at[tuple(neighbour)].set(high)


def block_scale(stream_key, dims, shards, smallest, largest):
    def one(dim, blocks):
        steps = jax.random.uniform(jax.random.fold_in(jax.random.fold_in(stream_key, 6), dim), (blocks,), jnp.float32, smallest / len(shards), largest / len(shards))
        return jnp.repeat(jnp.exp(steps), dims[dim] // blocks).reshape((-1,) + (1,) * (len(dims) - dim - 1))

    factor_of = one(*shards[0])
    for cut in shards[1:]:
        factor_of = factor_of * one(*cut)
    return factor_of


def rank_table(amount, skew):
    portions = [(1 << 20) // math.isqrt(grade ** skew) + 1 for grade in range(1, amount + 1)]
    spread = 1 + sum(portions) // (1 << 30)
    return np.cumsum(np.array([max(1, weight // spread) for weight in portions]))


def ranked_ids(rng, shape, amount, skew):
    table = rank_table(amount, skew)
    lot = jax.random.randint(jax.random.fold_in(rng, 1), shape, 0, int(table[amount - 1]))
    grade = jnp.searchsorted(jnp.asarray(table, jnp.int32), lot, side="right")
    return jax.random.permutation(jax.random.fold_in(rng, 2), amount)[grade].astype(jnp.int32)


def gaussian(rng, extent, scale, most, pieces=(), held_as=jnp.bfloat16):
    level = block_scale(rng, extent, pieces, -0.22, 0.18) if pieces else 1.0
    drawn = jax.random.normal(rng, extent, jnp.float32) * scale * level
    return jnp.minimum(jnp.maximum(drawn, -most), most).astype(held_as)


def setup_inputs(seed: int = 0) -> dict:
    splits = jax.random.split(jax.random.key(seed), 13)
    return {
        "q_noised": draw_q_noised(jax.random.fold_in(splits[12], 71), 0),
        "key_clean": draw_key_clean(jax.random.fold_in(splits[12], 71), 0),
        "value_clean": gaussian(splits[2], (TOKENS, KV_WIDTH), 1.0, 5.0, ((0, 8), (1, 4))),
        "key_noised": gaussian(splits[3], (TOKENS, KV_WIDTH), 1.0, 5.0, ((0, 8), (1, 4))),
        "value_noised": gaussian(splits[4], (TOKENS, KV_WIDTH), 1.0, 5.0, ((0, 8), (1, 4))),
        "out_weight": gaussian(splits[5], (D, D), D ** -0.5, 0.09375, ((0, 4),)),
        "residual": draw_residual(jax.random.fold_in(splits[12], 71), 0),
        "norm_gain": jnp.clip(1.0 + 0.1 * jax.random.normal(splits[7], (D,), jnp.float32), 0.5, 1.5),
        "head_weight": draw_head_weight(jax.random.fold_in(splits[12], 71), 0),
        "targets": plant(ranked_ids(splits[9], (TOKENS,), VOCAB, 2), jax.random.fold_in(splits[9], 3), 0, VOCAB - 1).astype(jnp.int32),
        "mask_flags": draw_mask_flags(jax.random.fold_in(splits[12], 71), 0),
        "levels": draw_levels(jax.random.fold_in(splits[12], 71), 0),
    }


very_low = -1e+30
norm_eps = 1e-06

def reference(q_noised, key_clean, value_clean, key_noised, value_noised, out_weight, residual, norm_gain, head_weight, targets, mask_flags, levels):
    scale = HEAD_DIM ** (-0.5)
    group = HEADS // KV_HEADS
    blocks = jnp.arange(TOKENS) // BLOCK
    earlier = blocks[None, :] < blocks[:, None]
    same = blocks[None, :] == blocks[:, None]

    def split_heads(array, count):
        return array.reshape(TOKENS, count, HEAD_DIM).transpose(1, 0, 2)

    def widen(array):
        return jnp.repeat(split_heads(array, KV_HEADS), group, axis=0)

    def one_head(parts):
        query, key_c, val_c, key_n, val_n = parts
        clean_scores = jnp.where(earlier, jnp.dot(query, key_c.T, preferred_element_type=jnp.float32) * scale, very_low)
        noised_scores = jnp.where(same, jnp.dot(query, key_n.T, preferred_element_type=jnp.float32) * scale, very_low)
        top = jnp.maximum(lax.optimization_barrier(jnp.max(clean_scores, axis=1)), lax.optimization_barrier(jnp.max(noised_scores, axis=1)))
        clean_w = jnp.exp(clean_scores - top[:, None])
        noised_w = jnp.exp(noised_scores - top[:, None])
        denominator = lax.optimization_barrier(jnp.sum(clean_w, axis=1)) + lax.optimization_barrier(jnp.sum(noised_w, axis=1))
        numerator = jnp.dot(clean_w.astype(jnp.bfloat16), val_c, preferred_element_type=jnp.float32)
        numerator = numerator + jnp.dot(noised_w.astype(jnp.bfloat16), val_n, preferred_element_type=jnp.float32)
        return (numerator / denominator[:, None]).astype(jnp.bfloat16)
    parts = (split_heads(q_noised, HEADS), widen(key_clean), widen(value_clean), widen(key_noised), widen(value_noised))
    heads_out = lax.map(one_head, parts)
    attention = heads_out.transpose(1, 0, 2).reshape(TOKENS, D)
    projected = jnp.dot(attention, out_weight, preferred_element_type=jnp.float32)
    hidden = residual.astype(jnp.float32) + projected
    normed = (hidden * lax.rsqrt(lax.optimization_barrier(jnp.mean(hidden * hidden, axis=1, keepdims=True)) + norm_eps) * norm_gain).astype(jnp.bfloat16)
    total_slots = N_SEQ * CAP
    order = jnp.argsort(1 - mask_flags, stable=True)[:total_slots].astype(jnp.int32)
    rows_sel = normed[order].reshape(N_SEQ, CAP, D)
    wanted_sel = targets[order].reshape(N_SEQ, CAP)

    def row_loss(parts_rows):
        rows, wanted = parts_rows
        logits = lax.dot_general(rows, head_weight, (((1,), (1,)), ((), ())), preferred_element_type=jnp.float32)
        top = lax.optimization_barrier(jnp.max(logits, axis=1))
        log_total = top + jnp.log(lax.optimization_barrier(jnp.sum(jnp.exp(logits - top[:, None]), axis=1)))
        picked = jnp.take_along_axis(logits, wanted[:, None], axis=1)[:, 0]
        return log_total - picked
    nll = lax.map(row_loss, (rows_sel, wanted_sel)).reshape(total_slots)
    nll = jnp.where(mask_flags[order] == 1, nll, 0.0)
    per_token = jnp.zeros((TOKENS,), jnp.float32).at[order].set(nll)
    return per_token / (levels[blocks] + 1).astype(jnp.float32)
```

```python
import jax
import jax.numpy as jnp
from jax import lax
from jax.sharding import PartitionSpec as P

D = 4096
HEAD_DIM = 128
BLOCK = 32
CAP = 48

very_low = -1e30
norm_eps = 1e-06


def shards(
    q_noised,
    key_clean,
    value_clean,
    key_noised,
    value_noised,
    out_weight,
    residual,
    norm_gain,
    head_weight,
    targets,
    mask_flags,
    levels,
):
    tok_rows, q_width = q_noised.shape
    width = residual.shape[1]
    heads_local = q_width // HEAD_DIM
    kv_local = key_clean.shape[1] // HEAD_DIM
    group = heads_local // kv_local
    vocab_rows = head_weight.shape[0]
    S = lax.axis_size("seq")
    V = lax.axis_size("vocab")
    C = 2
    X = V // C
    Y = 2
    Z = S // Y
    HALF = CAP // C
    share = width // X
    seq_index = lax.axis_index("seq")
    vocab_index = lax.axis_index("vocab")
    z, y = seq_index // Y, seq_index % Y
    x, c = vocab_index // C, vocab_index % C
    first_row = seq_index * tok_rows
    scale = HEAD_DIM ** (-0.5)

    def dev(zi, yi, xi, ci):
        return ((zi * Y + yi) * X + xi) * C + ci

    def permute(block, pairs):
        return lax.ppermute(block, ("seq", "vocab"), pairs)

    every = [(zi, yi, xi, ci) for zi in range(Z) for yi in range(Y) for xi in range(X) for ci in range(C)]

    def core_flip(block):
        return permute(block, [(dev(a, b, e, f), dev(a, b, e, 1 - f)) for a, b, e, f in every])

    def x_shift(block, k):
        return permute(block, [(dev(a, b, e, f), dev(a, b, (e + k) % X, f)) for a, b, e, f in every])

    def y_flip(block):
        return permute(block, [(dev(a, b, e, f), dev(a, 1 - b, e, f)) for a, b, e, f in every])

    def z_up(block, k):
        return permute(block, [(dev(a, b, e, f), dev(a + k, b, e, f)) for a, b, e, f in every if a + k < Z])

    def z_shift(block, k):
        return permute(block, [(dev(a, b, e, f), dev((a + k) % Z, b, e, f)) for a, b, e, f in every])

    def mixed_flip(block, first):
        pairs = []
        for a, b, e, f in every:
            if (f == 0) == first:
                pairs.append((dev(a, b, e, f), dev(a, b, 1 - e, f)))
            else:
                pairs.append((dev(a, b, e, f), dev(a, 1 - b, e, f)))
        return permute(block, pairs)

    own_kv = jnp.stack([key_clean, value_clean])
    pieces = [(own_kv, seq_index)]
    pieces.append((y_flip(own_kv), z * Y + 1 - y))
    for k in range(1, Z):
        got = z_up(own_kv, k)
        src = jnp.where(z >= k, (z - k) * Y, S)
        pieces.append((got, src + y))
        pieces.append((y_flip(got), src + 1 - y))
    other_head = core_flip(head_weight)

    all_mask = mask_flags.reshape(S, tok_rows)
    all_slot = jnp.cumsum(all_mask, axis=1) - 1
    slot_hit = (all_mask[:, None, :] == 1) & (all_slot[:, None, :] == jnp.arange(CAP)[None, :, None])
    slot_targets = jnp.sum(jnp.where(slot_hit, targets.reshape(S, 1, tok_rows), 0), axis=2)
    my_mask = lax.dynamic_slice_in_dim(mask_flags, first_row, tok_rows)
    my_slot = jnp.cumsum(my_mask) - 1
    chosen = (my_mask[None, :] == 1) & (my_slot[None, :] == jnp.arange(CAP)[:, None])
    selector = chosen.astype(jnp.bfloat16)
    local_block = jnp.arange(tok_rows) // BLOCK
    slot_block = jnp.sum(jnp.where(chosen, local_block[None, :], 0), axis=1)
    query_block = slot_block + first_row // BLOCK
    rows_block = jnp.tile(query_block, group)
    rows_local = jnp.tile(slot_block, group)
    queries = jnp.dot(selector, q_noised, preferred_element_type=jnp.float32).astype(jnp.bfloat16)
    residual_sel = jnp.dot(selector, residual, preferred_element_type=jnp.float32)

    heads_out = []
    for g in range(kv_local):
        cols = slice(g * HEAD_DIM, (g + 1) * HEAD_DIM)
        q_g = jnp.concatenate(
            [queries[:, (g * group + h) * HEAD_DIM : (g * group + h + 1) * HEAD_DIM] for h in range(group)]
        )

        def attend(keys, visible):
            scores = lax.dot_general(q_g, keys, (((1,), (1,)), ((), ())), preferred_element_type=jnp.float32)
            return jnp.where(visible, scores * scale, very_low)

        parts = [attend(key_noised[:, cols], local_block[None, :] == rows_local[:, None])]
        values = [value_noised[:, cols]]
        for kv, src in pieces:
            key_block = src * (tok_rows // BLOCK) + local_block
            parts.append(attend(kv[0][:, cols], key_block[None, :] < rows_block[:, None]))
            values.append(kv[1][:, cols])
        scores = jnp.concatenate(parts, axis=1)
        top = jnp.max(scores, axis=1, keepdims=True)
        weights = jnp.exp(scores - top)
        total = jnp.sum(weights, axis=1, keepdims=True)
        out = jnp.dot(weights.astype(jnp.bfloat16), jnp.concatenate(values), preferred_element_type=jnp.float32)
        out = (out / total).astype(jnp.bfloat16)
        heads_out += [out[h * CAP : (h + 1) * CAP] for h in range(group)]
    attention = jnp.concatenate(heads_out, axis=1)
    projected = jnp.dot(attention, out_weight, preferred_element_type=jnp.float32)

    mine = lax.dynamic_slice_in_dim(projected, c * HALF, HALF)
    theirs = lax.dynamic_slice_in_dim(projected, (1 - c) * HALF, HALF).astype(jnp.bfloat16)
    mine = mine + core_flip(theirs).astype(jnp.float32)
    sent = mine.astype(jnp.bfloat16)
    summed = sent.astype(jnp.float32)
    for k in range(1, X):
        summed = summed + x_shift(sent, k).astype(jnp.float32)
    hidden = lax.dynamic_slice_in_dim(residual_sel, c * HALF, HALF) + summed
    squares = jnp.sum(hidden * hidden, axis=1, keepdims=True)
    normed = (hidden * lax.rsqrt(squares / D + norm_eps) * norm_gain[None, :]).astype(jnp.bfloat16)

    own = lax.dynamic_slice_in_dim(normed, x * share, share, 1)
    slabs = [own] + [z_shift(own, k) for k in range(1, Z)]
    column = jnp.stack(slabs)
    if X == Y:
        step1 = mixed_flip(column, True)
        both = jnp.stack([column, step1])
        step2 = mixed_flip(both, False)
        quad = jnp.stack([both, step2])
        quad = jnp.where(c == 0, quad, jnp.swapaxes(quad, 0, 1))
        by_x = [quad[:, d] for d in range(X)]
    else:
        pair = jnp.stack([column, y_flip(column)])
        by_x = [pair] + [x_shift(pair, k) for k in range(1, X)]
    stackx = jnp.stack(by_x)
    n_rows = Y * Z * HALF
    order_x = (x - jnp.arange(X)) % X
    logits = []
    for w in (head_weight, other_head):
        total = None
        for k in range(X):
            w_k = lax.dynamic_slice_in_dim(w, ((x - k) % X) * share, share, 1)
            part = lax.dot_general(
                stackx[k].reshape(n_rows, share), w_k, (((1,), (1,)), ((), ())), preferred_element_type=jnp.float32
            )
            total = part if total is None else total + part
        logits.append(total)
    src_y = jnp.stack([y, 1 - y])
    src_z = (z - jnp.arange(Z)) % Z
    src_s = (src_z[None, :] * Y + src_y[:, None]).reshape(Y * Z)
    to_s = (src_s[None, :] == jnp.arange(S)[:, None])
    half_targets = lax.dynamic_slice_in_dim(slot_targets, c * HALF, HALF, 1)
    row_targets = jnp.sum(jnp.where(to_s[:, :, None], half_targets[:, None, :], 0), axis=0).reshape(n_rows)
    first = (seq_index * V + x * C) * vocab_rows
    base = [first + c * vocab_rows, first + (1 - c) * vocab_rows]
    row_top = jnp.maximum(jnp.max(logits[0], axis=1), jnp.max(logits[1], axis=1))
    row_total = 0.0
    row_pick = 0.0
    for b, lg in zip(base, logits):
        row_total = row_total + jnp.sum(jnp.exp(lg - row_top[:, None]), axis=1)
        ids = b + jnp.arange(vocab_rows)
        row_pick = row_pick + jnp.sum(jnp.where(ids[None, :] == row_targets[:, None], lg, 0.0), axis=1)
    row_lse = row_top + jnp.log(row_total)
    stats = jnp.concatenate([row_lse.reshape(S, HALF), row_pick.reshape(S, HALF)], axis=1)
    stats = jnp.sum(jnp.where(to_s[:, :, None], stats[None], 0.0), axis=1)
    stats = jnp.pad(stats, ((0, 0), (0, 128 - 2 * HALF)))
    send = jnp.broadcast_to(stats[:, None], (S, V, 128)).reshape(S * V, 128)
    got = lax.all_to_all(send, ("seq", "vocab"), 0, 0, tiled=True).reshape(S * X, C, 128)
    lse = got[:, :, :HALF]
    picked = jnp.sum(got[:, :, HALF : 2 * HALF], axis=0).reshape(CAP)
    best = jnp.max(lse, axis=0)
    nll = (best + jnp.log(jnp.sum(jnp.exp(lse - best[None]), axis=0))).reshape(CAP) - picked
    token_nll = jnp.sum(jnp.where(chosen, nll[:, None], 0.0), axis=0)
    my_levels = lax.dynamic_slice_in_dim(levels, seq_index * (tok_rows // BLOCK), tok_rows // BLOCK)
    token_level = jnp.repeat(my_levels, BLOCK)
    return token_nll / (token_level + 1).astype(jnp.float32)


def solution(mesh):
    in_specs = (
        P("seq", "vocab"),
        P("seq", "vocab"),
        P("seq", "vocab"),
        P("seq", "vocab"),
        P("seq", "vocab"),
        P("vocab", None),
        P("seq", None),
        P(),
        P(("seq", "vocab"), None),
        P(),
        P(),
        P(),
    )
    return jax.shard_map(shards, mesh=mesh, in_specs=in_specs, out_specs=P("seq"), check_vma=False)
```

```python
import functools

import jax
import jax.numpy as jnp
from jax import lax
from jax.experimental import pallas as pl
from jax.experimental.pallas import tpu as pltpu
from jax.sharding import PartitionSpec as P

D = 4096
HEAD_DIM = 128
BLOCK = 32
CAP = 48
LANES = 128
SHIFT = BLOCK.bit_length() - 1

very_low = -1e30
norm_eps = 1e-06

VMEM = pl.BlockSpec(memory_space=pltpu.VMEM)
SMEM = pl.BlockSpec(memory_space=pltpu.SMEM)
NT = (((1,), (1,)), ((), ()))


def call(kernel, name, outs, n_smem, args, mib, flops=0, scratch=()):
    n_bytes = sum(a.size * a.dtype.itemsize for a in args)
    return pl.pallas_call(
        kernel,
        out_shape=outs,
        in_specs=[SMEM] * n_smem + [VMEM] * (len(args) - n_smem),
        out_specs=jax.tree.map(lambda _: VMEM, outs),
        scratch_shapes=list(scratch),
        compiler_params=pltpu.CompilerParams(vmem_limit_bytes=mib << 20),
        cost_estimate=pl.CostEstimate(flops=flops, bytes_accessed=n_bytes, transcendentals=0),
        name=name,
    )(*args)


def select_kernel(where_ref, mask_ref, q_ref, res_ref, q_out, res_out, blk_out):
    tok = mask_ref.shape[1]
    before = lax.broadcasted_iota(jnp.int32, (tok, tok), 0) <= lax.broadcasted_iota(jnp.int32, (tok, tok), 1)
    upto = before.astype(jnp.float32)
    slots = lax.broadcasted_iota(jnp.int32, (CAP, tok), 0).astype(jnp.float32)
    block = lax.shift_right_logical(lax.broadcasted_iota(jnp.int32, (CAP, tok), 1), SHIFT).astype(jnp.float32)
    for which in range(2):
        row = mask_ref[pl.ds(where_ref[which], 1), :].astype(jnp.float32)
        count = jnp.dot(jnp.broadcast_to(row, (8, tok)), upto, preferred_element_type=jnp.float32)[0:1]
        chosen = ((count - 1.0) == slots) & (row == 1.0)
        pick = jnp.where(chosen, 1.0, 0.0)
        blk_out[which] = jnp.broadcast_to(jnp.sum(pick * block, axis=1, keepdims=True), (CAP, LANES))
        if which == 0:
            pick = pick.astype(jnp.bfloat16)
            q_out[...] = jnp.dot(pick, q_ref[...], preferred_element_type=jnp.float32).astype(jnp.bfloat16)
            res_out[...] = jnp.dot(pick, res_ref[...], preferred_element_type=jnp.float32).astype(jnp.bfloat16)


def split3(value):
    high = value.astype(jnp.bfloat16).astype(jnp.float32)
    rest = value - high
    mid = rest.astype(jnp.bfloat16).astype(jnp.float32)
    return high, mid, rest - mid


def attend_kernel(n_pieces, heads, kv_heads, where_ref, blk_ref, q_own, q_other, kn_ref, vn_ref, *refs):
    pieces, (own_out, own_lse, other_out) = refs[:n_pieces], refs[n_pieces:]
    group = heads // kv_heads
    tok = kn_ref.shape[0]
    per_dev = tok // BLOCK
    scale = HEAD_DIM ** (-0.5)
    lane = lax.broadcasted_iota(jnp.int32, (CAP, LANES), 1)
    key_block = lax.shift_right_logical(lax.broadcasted_iota(jnp.int32, (CAP, tok), 1), SHIFT)
    for which in range(2):
        q_ref = (q_own, q_other)[which]
        slot_block = blk_ref[which][:, :1].astype(jnp.int32)
        row_block = slot_block + where_ref[which] * per_dev
        bias = []
        for k in range(n_pieces):
            seen = (key_block + where_ref[2 + k] * per_dev) < row_block
            bias.append(jnp.concatenate([jnp.where(seen, 0.0, very_low)] * group, axis=0))
        if which == 0:
            bias.append(jnp.concatenate([jnp.where(key_block == slot_block, 0.0, very_low)] * group, axis=0))
        lse_all = jnp.zeros((CAP, LANES), jnp.float32)
        for g in range(kv_heads):
            cols = slice(g * HEAD_DIM, (g + 1) * HEAD_DIM)
            q_g = jnp.concatenate(
                [q_ref[:, (g * group + h) * HEAD_DIM : (g * group + h + 1) * HEAD_DIM] for h in range(group)], axis=0
            )
            keys = [p[0][:, cols] for p in pieces]
            values = [p[1][:, cols] for p in pieces]
            if which == 0:
                keys.append(kn_ref[:, cols])
                values.append(vn_ref[:, cols])
            scores = [
                lax.dot_general(q_g, k, NT, preferred_element_type=jnp.float32) * scale + b for k, b in zip(keys, bias)
            ]
            top = functools.reduce(jnp.maximum, scores)
            top = jnp.max(top, axis=1, keepdims=True)
            weights = [jnp.exp(s - top) for s in scores]
            total = jnp.sum(functools.reduce(jnp.add, weights), axis=1, keepdims=True)
            mixed = functools.reduce(
                jnp.add,
                [jnp.dot(w.astype(jnp.bfloat16), v, preferred_element_type=jnp.float32) for w, v in zip(weights, values)],
            )
            mixed = mixed / total
            lse = top + jnp.log(total)
            for h in range(group):
                head = g * group + h
                rows = slice(h * CAP, (h + 1) * CAP)
                at = slice(head * HEAD_DIM, (head + 1) * HEAD_DIM)
                lse_all = jnp.where(lane == head, lse[rows], lse_all)
                if which == 0:
                    own_out[:, at] = mixed[rows]
                else:
                    other_out[:, at] = mixed[rows].astype(jnp.bfloat16)
        if which == 0:
            own_lse[...] = lse_all
        else:
            high, mid, low = split3(lse_all)
            packed = high + pltpu.roll(mid, 32, 1) + pltpu.roll(low, 64, 1)
            other_out[:, heads * HEAD_DIM :] = packed.astype(jnp.bfloat16)


def project_kernel(heads, where_ref, own_ref, lse_ref, got_ref, w_ref, mine_out, theirs_out):
    half = CAP // 2
    packed = got_ref[:, heads * HEAD_DIM :].astype(jnp.float32)
    got_lse = packed + pltpu.roll(packed, LANES - 32, 1) + pltpu.roll(packed, LANES - 64, 1)
    own_lse = lse_ref[...]
    top = jnp.maximum(own_lse, got_lse)
    w_own, w_got = jnp.exp(own_lse - top), jnp.exp(got_lse - top)
    total = w_own + w_got
    w_own, w_got = w_own / total, w_got / total
    parts = []
    for h in range(heads):
        at = slice(h * HEAD_DIM, (h + 1) * HEAD_DIM)
        joined = own_ref[:, at] * w_own[:, h : h + 1] + got_ref[:, at].astype(jnp.float32) * w_got[:, h : h + 1]
        parts.append(joined.astype(jnp.bfloat16))
    attention = jnp.concatenate(parts, axis=1)
    first = where_ref[0] == 0
    width = w_ref.shape[1]
    step = min(1024, width)
    for j in range(0, width, step):
        out = jnp.dot(attention, w_ref[:, j : j + step], preferred_element_type=jnp.float32)
        upper, lower = out[:half], out[half:]
        mine_out[:, j : j + step] = jnp.where(first, upper, lower)
        theirs_out[:, j : j + step] = jnp.where(first, lower, upper).astype(jnp.bfloat16)


def logits_kernel(mixed, X, Y, Z, V, where_ref, target_ref, *refs):
    half = CAP // 2
    share = refs[0].shape[1]
    n_rows = Y * Z * half
    quarter = Z * half
    if mixed:
        column, step1, step2, w_own, w_other, out_ref, near, far = refs

        @pl.when(where_ref[1] == 0)
        def _():
            near[quarter:] = step2[:quarter]
            far[:quarter] = step1[...]

        @pl.when(where_ref[1] != 0)
        def _():
            near[quarter:] = step1[...]
            far[:quarter] = step2[:quarter]

        near[:quarter] = column[...]
        far[quarter:] = step2[quarter:]
        rows = [near, far]
    else:
        rows = refs[:X]
        w_own, w_other, out_ref = refs[X:]
    logits = []
    for w in (w_own, w_other):
        total = None
        for k in range(X):
            at = pl.multiple_of(lax.rem(where_ref[0] + (X - k), X) * share, LANES)
            part = lax.dot_general(w[:, pl.ds(at, share)], rows[k][...], NT, preferred_element_type=jnp.float32)
            total = part if total is None else total + part
        logits.append(total)
    top = jnp.maximum(jnp.max(logits[0], axis=0, keepdims=True), jnp.max(logits[1], axis=0, keepdims=True))
    summed = 0.0
    picked = 0.0
    for i, lg in enumerate(logits):
        ids = lax.broadcasted_iota(jnp.int32, lg.shape, 0) + where_ref[2 + i]
        summed = summed + jnp.sum(jnp.exp(lg - top), axis=0, keepdims=True)
        picked = picked + jnp.sum(jnp.where(ids == target_ref[...], lg, 0.0), axis=0, keepdims=True)
    lse = top + jnp.log(summed)
    wide = -(-n_rows // LANES) * LANES
    pad = [jnp.zeros((1, wide - n_rows), jnp.float32)] if wide > n_rows else []
    lse = jnp.broadcast_to(jnp.concatenate([lse, *pad], axis=1), (8, wide))
    picked = jnp.broadcast_to(jnp.concatenate([picked, *pad], axis=1), (8, wide))
    lane = lax.broadcasted_iota(jnp.int32, (8, LANES), 1)
    for p in range(Y * Z):
        a = pltpu.roll(lse, (wide - p * half) % wide, 1)[:, :LANES]
        b = pltpu.roll(picked, (wide - p * half + half) % wide, 1)[:, :LANES]
        row = jnp.where(lane < half, a, b)[0:1]
        first = where_ref[4 + p] * V
        for v in range(V):
            out_ref[first + v] = row


def shards(
    q_noised,
    key_clean,
    value_clean,
    key_noised,
    value_noised,
    out_weight,
    residual,
    norm_gain,
    head_weight,
    targets,
    mask_flags,
    levels,
):
    tok_rows, q_width = q_noised.shape
    width = residual.shape[1]
    heads_local = q_width // HEAD_DIM
    kv_local = key_clean.shape[1] // HEAD_DIM
    vocab_rows = head_weight.shape[0]
    S = lax.axis_size("seq")
    V = lax.axis_size("vocab")
    C = 2
    X = V // C
    Y = 2
    Z = S // Y
    HALF = CAP // C
    share = width // X
    seq_index = lax.axis_index("seq")
    vocab_index = lax.axis_index("vocab")
    z, y = seq_index // Y, seq_index % Y
    x, c = vocab_index // C, vocab_index % C
    first_row = seq_index * tok_rows

    def dev(zi, yi, xi, ci):
        return ((zi * Y + yi) * X + xi) * C + ci

    def permute(block, pairs):
        return lax.ppermute(block, ("seq", "vocab"), pairs)

    every = [(zi, yi, xi, ci) for zi in range(Z) for yi in range(Y) for xi in range(X) for ci in range(C)]

    def core_flip(block):
        return permute(block, [(dev(a, b, e, f), dev(a, b, e, 1 - f)) for a, b, e, f in every])

    def x_shift(block, k):
        return permute(block, [(dev(a, b, e, f), dev(a, b, (e + k) % X, f)) for a, b, e, f in every])

    def y_flip(block):
        return permute(block, [(dev(a, b, e, f), dev(a, 1 - b, e, f)) for a, b, e, f in every])

    def z_up(block, k):
        return permute(block, [(dev(a, b, e, f), dev(a + k, b, e, f)) for a, b, e, f in every if a + k < Z])

    def z_shift(block, k):
        return permute(block, [(dev(a, b, e, f), dev((a + k) % Z, b, e, f)) for a, b, e, f in every])

    def mixed_flip(block, first):
        pairs = []
        for a, b, e, f in every:
            if (f == 0) == first:
                pairs.append((dev(a, b, e, f), dev(a, b, 1 - e, f)))
            else:
                pairs.append((dev(a, b, e, f), dev(a, 1 - b, e, f)))
        return permute(block, pairs)

    def scalars(*values):
        return jnp.stack([jnp.asarray(v, jnp.int32) for v in values])

    own_kv = jnp.stack([key_clean, value_clean])
    pieces, sources = [own_kv], [seq_index]
    for k in range(1, Z):
        pieces.append(z_up(own_kv, k))
        sources.append(jnp.where(z >= k, (z - k) * Y + y, S))
    partner = z * Y + 1 - y
    all_mask = mask_flags.reshape(S, tok_rows)
    queries, residual_sel, slot_blocks = call(
        select_kernel,
        "select_rows",
        (
            jax.ShapeDtypeStruct((CAP, q_width), jnp.bfloat16),
            jax.ShapeDtypeStruct((CAP, width), jnp.bfloat16),
            jax.ShapeDtypeStruct((2, CAP, LANES), jnp.float32),
        ),
        1,
        (scalars(seq_index, partner), all_mask, q_noised, residual),
        8,
    )
    other_queries = y_flip(queries)
    other_head = core_flip(head_weight)
    own_sum, own_lse, other_sum = call(
        functools.partial(attend_kernel, Z, heads_local, kv_local),
        "attend",
        (
            jax.ShapeDtypeStruct((CAP, q_width), jnp.float32),
            jax.ShapeDtypeStruct((CAP, LANES), jnp.float32),
            jax.ShapeDtypeStruct((CAP, q_width + LANES), jnp.bfloat16),
        ),
        1,
        (scalars(seq_index, partner, *sources), slot_blocks, queries, other_queries, key_noised, value_noised, *pieces),
        16,
    )
    got_sum = y_flip(other_sum)
    mine, theirs = call(
        functools.partial(project_kernel, heads_local),
        "project",
        (jax.ShapeDtypeStruct((HALF, width), jnp.float32), jax.ShapeDtypeStruct((HALF, width), jnp.bfloat16)),
        1,
        (scalars(c), own_sum, own_lse, got_sum, out_weight),
        16,
    )

    all_slot = jnp.cumsum(all_mask, axis=1) - 1
    slot_hit = (all_mask[:, None, :] == 1) & (all_slot[:, None, :] == jnp.arange(CAP)[None, :, None])
    slot_targets = jnp.sum(jnp.where(slot_hit, targets.reshape(S, 1, tok_rows), 0), axis=2)
    my_mask = lax.dynamic_slice_in_dim(mask_flags, first_row, tok_rows)
    my_slot = jnp.cumsum(my_mask) - 1
    chosen = (my_mask[None, :] == 1) & (my_slot[None, :] == jnp.arange(CAP)[:, None])

    mine = mine + core_flip(theirs).astype(jnp.float32)
    sent = mine.astype(jnp.bfloat16)
    summed = mine
    for k in range(1, X):
        summed = summed + x_shift(sent, k).astype(jnp.float32)
    hidden = lax.dynamic_slice_in_dim(residual_sel, c * HALF, HALF).astype(jnp.float32) + summed
    squares = jnp.sum(hidden * hidden, axis=1, keepdims=True)
    normed = (hidden * lax.rsqrt(squares / D + norm_eps) * norm_gain[None, :]).astype(jnp.bfloat16)

    own = lax.dynamic_slice_in_dim(normed, x * share, share, 1)
    slabs = [own] + [z_shift(own, k) for k in range(1, Z)]
    column = jnp.stack(slabs)
    n_rows = Y * Z * HALF
    mixed = X == Y
    if mixed:
        step1 = mixed_flip(column, True)
        step2 = mixed_flip(jnp.stack([column, step1]), False)
        rows = [column.reshape(Z * HALF, share), step1.reshape(Z * HALF, share), step2.reshape(n_rows, share)]
        scratch = [pltpu.VMEM((n_rows, share), jnp.bfloat16)] * 2
    else:
        pair = jnp.stack([column, y_flip(column)])
        rows = [pair.reshape(n_rows, share)] + [x_shift(pair, k).reshape(n_rows, share) for k in range(1, X)]
        scratch = []
    src_z = (z - jnp.arange(Z)) % Z
    src_s = (src_z[None, :] * Y + jnp.stack([y, 1 - y])[:, None]).reshape(Y * Z)
    from_s = src_s[None, :] == jnp.arange(S)[:, None]
    half_targets = lax.dynamic_slice_in_dim(slot_targets, c * HALF, HALF, 1)
    row_targets = jnp.sum(jnp.where(from_s[:, :, None], half_targets[:, None, :], 0), axis=0).reshape(1, n_rows)
    first = (seq_index * V + x * C) * vocab_rows
    send = call(
        functools.partial(logits_kernel, mixed, X, Y, Z, V),
        "logits",
        jax.ShapeDtypeStruct((S * V, 1, LANES), jnp.float32),
        1,
        (
            jnp.concatenate([scalars(x, c, first + c * vocab_rows, first + (1 - c) * vocab_rows), src_s.astype(jnp.int32)]),
            row_targets,
            *rows,
            head_weight,
            other_head,
        ),
        24,
        4 * n_rows * width * vocab_rows,
        scratch,
    ).reshape(S * V, LANES)
    got = lax.all_to_all(send, ("seq", "vocab"), 0, 0, tiled=True).reshape(S * X, C, LANES)
    lse = got[:, :, :HALF]
    picked = jnp.sum(got[:, :, HALF : 2 * HALF], axis=0).reshape(CAP)
    best = jnp.max(lse, axis=0)
    nll = (best + jnp.log(jnp.sum(jnp.exp(lse - best[None]), axis=0))).reshape(CAP) - picked
    token_nll = jnp.sum(jnp.where(chosen, nll[:, None], 0.0), axis=0)
    my_levels = lax.dynamic_slice_in_dim(levels, seq_index * (tok_rows // BLOCK), tok_rows // BLOCK)
    token_level = jnp.repeat(my_levels, BLOCK)
    return token_nll / (token_level + 1).astype(jnp.float32)


def solution(mesh):
    in_specs = (
        P("seq", "vocab"),
        P("seq", "vocab"),
        P("seq", "vocab"),
        P("seq", "vocab"),
        P("seq", "vocab"),
        P("vocab", None),
        P("seq", None),
        P(),
        P(("seq", "vocab"), None),
        P(),
        P(),
        P(),
    )
    return jax.shard_map(shards, mesh=mesh, in_specs=in_specs, out_specs=P("seq"), check_vma=False)
```

```python
import functools

import jax
import jax.numpy as jnp
from jax import lax
from jax.experimental import pallas as pl
from jax.experimental.pallas import tpu as pltpu
from jax.sharding import PartitionSpec as P

D = 4096
HEAD_DIM = 128
BLOCK = 32
CAP = 48
LANES = 128
SHIFT = BLOCK.bit_length() - 1

very_low = -1e30
norm_eps = 1e-06

VMEM = pl.BlockSpec(memory_space=pltpu.VMEM)
SMEM = pl.BlockSpec(memory_space=pltpu.SMEM)
ANY = pl.BlockSpec(memory_space=pl.ANY)
NT = (((1,), (1,)), ((), ()))
MIB = 1 << 20


def call(kernel, name, outs, n_smem, args, mib, flops=0, scratch=(), n_any=0):
    n_bytes = sum(a.size * a.dtype.itemsize for a in args)
    return pl.pallas_call(
        kernel,
        out_shape=outs,
        in_specs=[SMEM] * n_smem + [VMEM] * (len(args) - n_smem - n_any) + [ANY] * n_any,
        out_specs=jax.tree.map(lambda _: VMEM, outs),
        scratch_shapes=list(scratch),
        compiler_params=pltpu.CompilerParams(vmem_limit_bytes=mib * MIB),
        cost_estimate=pl.CostEstimate(flops=flops, bytes_accessed=n_bytes, transcendentals=0),
        name=name,
    )(*args)


def slots_of(row):
    tok = row.shape[1]
    upto = lax.broadcasted_iota(jnp.int32, (tok, tok), 0) <= lax.broadcasted_iota(jnp.int32, (tok, tok), 1)
    row = row.astype(jnp.float32)
    count = jnp.dot(jnp.broadcast_to(row, (8, tok)), upto.astype(jnp.float32), preferred_element_type=jnp.float32)[0:1]
    slots = lax.broadcasted_iota(jnp.int32, (CAP, tok), 0).astype(jnp.float32)
    return ((count - 1.0) == slots) & (row == 1.0)


def select_kernel(where_ref, mask_ref, q_hbm, kn_hbm, vn_hbm, q_out, blk_out, kn_out, vn_out, q_ref, sems):
    copies = [
        pltpu.make_async_copy(src, dst, sems.at[i])
        for i, (src, dst) in enumerate(((q_hbm, q_ref), (kn_hbm, kn_out), (vn_hbm, vn_out)))
    ]
    for copy in copies:
        copy.start()
    tok = mask_ref.shape[1]
    block = lax.shift_right_logical(lax.broadcasted_iota(jnp.int32, (CAP, tok), 1), SHIFT).astype(jnp.float32)
    picks = []
    for which in range(2):
        pick = jnp.where(slots_of(mask_ref[pl.ds(where_ref[which], 1), :]), 1.0, 0.0)
        blk_out[which] = jnp.broadcast_to(jnp.sum(pick * block, axis=1, keepdims=True), (CAP, LANES))
        picks.append(pick)
    copies[0].wait()
    q_out[...] = jnp.dot(picks[0].astype(jnp.bfloat16), q_ref[...], preferred_element_type=jnp.float32).astype(jnp.bfloat16)
    copies[1].wait()
    copies[2].wait()


def stage_out_kernel(where_ref, mask_ref, res_hbm, w_hbm, after, res_out, w_out, res_ref, sems):
    whole = pltpu.make_async_copy(w_hbm, w_out, sems.at[0])
    whole.start()
    copy = pltpu.make_async_copy(res_hbm, res_ref, sems.at[1])
    copy.start()
    pick = jnp.where(slots_of(mask_ref[pl.ds(where_ref[0], 1), :]), 1.0, 0.0).astype(jnp.bfloat16)
    copy.wait()
    res_out[...] = jnp.dot(pick, res_ref[...], preferred_element_type=jnp.float32).astype(jnp.bfloat16)
    whole.wait()


def stage_head_kernel(own_hbm, other_hbm, after, own_out, other_out, sems):
    copies = [
        pltpu.make_async_copy(src, dst, sems.at[i])
        for i, (src, dst) in enumerate(((own_hbm, own_out), (other_hbm, other_out)))
    ]
    for copy in copies:
        copy.start()
    for copy in copies:
        copy.wait()


def split3(value):
    high = value.astype(jnp.bfloat16).astype(jnp.float32)
    rest = value - high
    mid = rest.astype(jnp.bfloat16).astype(jnp.float32)
    return high, mid, rest - mid


def attend_kernel(n_pieces, heads, kv_heads, where_ref, blk_ref, q_own, q_other, kn_ref, vn_ref, *refs):
    pieces, (own_out, own_lse, other_out) = refs[:n_pieces], refs[n_pieces:]
    group = heads // kv_heads
    tok = kn_ref.shape[0]
    per_dev = tok // BLOCK
    scale = HEAD_DIM ** (-0.5)
    lane = lax.broadcasted_iota(jnp.int32, (CAP, LANES), 1)
    key_block = lax.shift_right_logical(lax.broadcasted_iota(jnp.int32, (CAP, tok), 1), SHIFT)
    for which in range(2):
        q_ref = (q_own, q_other)[which]
        slot_block = blk_ref[which][:, :1].astype(jnp.int32)
        row_block = slot_block + where_ref[which] * per_dev
        bias = []
        for k in range(n_pieces):
            seen = (key_block + where_ref[2 + k] * per_dev) < row_block
            bias.append(jnp.concatenate([jnp.where(seen, 0.0, very_low)] * group, axis=0))
        if which == 0:
            bias.append(jnp.concatenate([jnp.where(key_block == slot_block, 0.0, very_low)] * group, axis=0))
        lse_all = jnp.zeros((CAP, LANES), jnp.float32)
        for g in range(kv_heads):
            cols = slice(g * HEAD_DIM, (g + 1) * HEAD_DIM)
            q_g = jnp.concatenate(
                [q_ref[:, (g * group + h) * HEAD_DIM : (g * group + h + 1) * HEAD_DIM] for h in range(group)], axis=0
            )
            keys = [p[0][:, cols] for p in pieces]
            values = [p[1][:, cols] for p in pieces]
            if which == 0:
                keys.append(kn_ref[:, cols])
                values.append(vn_ref[:, cols])
            scores = [
                lax.dot_general(q_g, k, NT, preferred_element_type=jnp.float32) * scale + b for k, b in zip(keys, bias)
            ]
            top = functools.reduce(jnp.maximum, scores)
            top = jnp.max(top, axis=1, keepdims=True)
            weights = [jnp.exp(s - top) for s in scores]
            total = jnp.sum(functools.reduce(jnp.add, weights), axis=1, keepdims=True)
            mixed = functools.reduce(
                jnp.add,
                [jnp.dot(w.astype(jnp.bfloat16), v, preferred_element_type=jnp.float32) for w, v in zip(weights, values)],
            )
            mixed = mixed / total
            lse = top + jnp.log(total)
            for h in range(group):
                head = g * group + h
                rows = slice(h * CAP, (h + 1) * CAP)
                at = slice(head * HEAD_DIM, (head + 1) * HEAD_DIM)
                lse_all = jnp.where(lane == head, lse[rows], lse_all)
                if which == 0:
                    own_out[:, at] = mixed[rows]
                else:
                    other_out[:, at] = mixed[rows].astype(jnp.bfloat16)
        if which == 0:
            own_lse[...] = lse_all
        else:
            high, mid, low = split3(lse_all)
            packed = high + pltpu.roll(mid, 32, 1) + pltpu.roll(low, 64, 1)
            other_out[:, heads * HEAD_DIM :] = packed.astype(jnp.bfloat16)


def project_kernel(heads, where_ref, own_ref, lse_ref, got_ref, w_ref, mine_out, theirs_out):
    half = CAP // 2
    packed = got_ref[:, heads * HEAD_DIM :].astype(jnp.float32)
    got_lse = packed + pltpu.roll(packed, LANES - 32, 1) + pltpu.roll(packed, LANES - 64, 1)
    own_lse = lse_ref[...]
    top = jnp.maximum(own_lse, got_lse)
    w_own, w_got = jnp.exp(own_lse - top), jnp.exp(got_lse - top)
    total = w_own + w_got
    w_own, w_got = w_own / total, w_got / total
    parts = []
    for h in range(heads):
        at = slice(h * HEAD_DIM, (h + 1) * HEAD_DIM)
        joined = own_ref[:, at] * w_own[:, h : h + 1] + got_ref[:, at].astype(jnp.float32) * w_got[:, h : h + 1]
        parts.append(joined.astype(jnp.bfloat16))
    attention = jnp.concatenate(parts, axis=1)
    first = where_ref[0] == 0
    width = w_ref.shape[1]
    step = min(1024, width)
    for j in range(0, width, step):
        out = jnp.dot(attention, w_ref[:, j : j + step], preferred_element_type=jnp.float32)
        upper, lower = out[:half], out[half:]
        mine_out[:, j : j + step] = jnp.where(first, upper, lower)
        theirs_out[:, j : j + step] = jnp.where(first, lower, upper).astype(jnp.bfloat16)


def logits_kernel(mixed, X, Y, sizes, V, where_ref, target_ref, *refs):
    half = CAP // 2
    share = refs[0].shape[1]
    n_rows = Y * sum(sizes) * half
    n_refs = (3 if mixed else X) * len(sizes)
    pieces, (w_own, w_other, out_ref, *rows) = refs[:n_refs], refs[n_refs:]
    base = 0
    for i, size in enumerate(sizes):
        n = size * half
        if mixed:
            column, step1, step2 = pieces[3 * i : 3 * i + 3]
            near, far = rows
            near[base : base + n] = column[...]
            far[base + n : base + 2 * n] = step2[n:]

            @pl.when(where_ref[1] == 0)
            def _(base=base, n=n, step1=step1, step2=step2):
                near[base + n : base + 2 * n] = step2[:n]
                far[base : base + n] = step1[...]

            @pl.when(where_ref[1] != 0)
            def _(base=base, n=n, step1=step1, step2=step2):
                near[base + n : base + 2 * n] = step1[...]
                far[base : base + n] = step2[:n]
        else:
            for k in range(X):
                rows[k][base : base + Y * n] = pieces[X * i + k][...]
        base += Y * n
    logits = []
    for w in (w_own, w_other):
        total = None
        for k in range(X):
            at = pl.multiple_of(lax.rem(where_ref[0] + (X - k), X) * share, LANES)
            part = lax.dot_general(w[:, pl.ds(at, share)], rows[k][...], NT, preferred_element_type=jnp.float32)
            total = part if total is None else total + part
        logits.append(total)
    top = jnp.maximum(jnp.max(logits[0], axis=0, keepdims=True), jnp.max(logits[1], axis=0, keepdims=True))
    summed = 0.0
    picked = 0.0
    for i, lg in enumerate(logits):
        ids = lax.broadcasted_iota(jnp.int32, lg.shape, 0) + where_ref[2 + i]
        summed = summed + jnp.sum(jnp.exp(lg - top), axis=0, keepdims=True)
        picked = picked + jnp.sum(jnp.where(ids == target_ref[...], lg, 0.0), axis=0, keepdims=True)
    lse = top + jnp.log(summed)
    wide = -(-n_rows // LANES) * LANES
    pad = [jnp.zeros((1, wide - n_rows), jnp.float32)] if wide > n_rows else []
    lse = jnp.broadcast_to(jnp.concatenate([lse, *pad], axis=1), (8, wide))
    picked = jnp.broadcast_to(jnp.concatenate([picked, *pad], axis=1), (8, wide))
    lane = lax.broadcasted_iota(jnp.int32, (8, LANES), 1)
    for p in range(Y * sum(sizes)):
        a = pltpu.roll(lse, (wide - p * half) % wide, 1)[:, :LANES]
        b = pltpu.roll(picked, (wide - p * half + half) % wide, 1)[:, :LANES]
        row = jnp.where(lane < half, a, b)[0:1]
        first = where_ref[4 + p] * V
        for v in range(V):
            out_ref[first + v] = row


def shards(
    q_noised,
    key_clean,
    value_clean,
    key_noised,
    value_noised,
    out_weight,
    residual,
    norm_gain,
    head_weight,
    targets,
    mask_flags,
    levels,
):
    tok_rows, q_width = q_noised.shape
    width = residual.shape[1]
    heads_local = q_width // HEAD_DIM
    kv_local = key_clean.shape[1] // HEAD_DIM
    vocab_rows = head_weight.shape[0]
    S = lax.axis_size("seq")
    V = lax.axis_size("vocab")
    C = 2
    X = V // C
    Y = 2
    Z = S // Y
    HALF = CAP // C
    share = width // X
    seq_index = lax.axis_index("seq")
    vocab_index = lax.axis_index("vocab")
    z, y = seq_index // Y, seq_index % Y
    x, c = vocab_index // C, vocab_index % C
    first_row = seq_index * tok_rows

    def dev(zi, yi, xi, ci):
        return ((zi * Y + yi) * X + xi) * C + ci

    def permute(block, pairs):
        return lax.ppermute(block, ("seq", "vocab"), pairs)

    every = [(zi, yi, xi, ci) for zi in range(Z) for yi in range(Y) for xi in range(X) for ci in range(C)]

    def core_flip(block):
        return permute(block, [(dev(a, b, e, f), dev(a, b, e, 1 - f)) for a, b, e, f in every])

    def x_shift(block, k):
        return permute(block, [(dev(a, b, e, f), dev(a, b, (e + k) % X, f)) for a, b, e, f in every])

    def y_flip(block):
        return permute(block, [(dev(a, b, e, f), dev(a, 1 - b, e, f)) for a, b, e, f in every])

    def z_up(block, k):
        return permute(block, [(dev(a, b, e, f), dev(a + k, b, e, f)) for a, b, e, f in every if a + k < Z])

    paired = Z & (Z - 1) == 0

    def z_swap(block, k):
        return permute(block, [(dev(a, b, e, f), dev(a ^ k if paired else (a + k) % Z, b, e, f)) for a, b, e, f in every])

    def from_z(k):
        return z ^ k if paired else (z - k) % Z

    def mixed_flip(block, first):
        pairs = []
        for a, b, e, f in every:
            if (f == 0) == first:
                pairs.append((dev(a, b, e, f), dev(a, b, 1 - e, f)))
            else:
                pairs.append((dev(a, b, e, f), dev(a, 1 - b, e, f)))
        return permute(block, pairs)

    def scalars(*values):
        return jnp.stack([jnp.asarray(v, jnp.int32) for v in values])

    own_kv = jnp.stack([key_clean, value_clean])
    pieces, sources = [own_kv], [seq_index]
    for k in range(1, Z):
        pieces.append(z_up(own_kv, k))
        sources.append(jnp.where(z >= k, (z - k) * Y + y, S))
    partner = z * Y + 1 - y
    all_mask = mask_flags.reshape(S, tok_rows)
    queries, slot_blocks, keys_here, values_here = call(
        select_kernel,
        "select_rows",
        (
            jax.ShapeDtypeStruct((CAP, q_width), jnp.bfloat16),
            jax.ShapeDtypeStruct((2, CAP, LANES), jnp.float32),
            jax.ShapeDtypeStruct(key_noised.shape, jnp.bfloat16),
            jax.ShapeDtypeStruct(value_noised.shape, jnp.bfloat16),
        ),
        1,
        (scalars(seq_index, partner), all_mask, q_noised, key_noised, value_noised),
        58,
        scratch=[pltpu.VMEM(q_noised.shape, jnp.bfloat16), pltpu.SemaphoreType.DMA((3,))],
        n_any=3,
    )
    residual_sel, staged_out = call(
        stage_out_kernel,
        "stage_out",
        (
            jax.ShapeDtypeStruct((CAP, width), jnp.bfloat16),
            jax.ShapeDtypeStruct(out_weight.shape, jnp.bfloat16),
        ),
        1,
        (scalars(seq_index), all_mask, residual, out_weight, slot_blocks),
        50,
        scratch=[pltpu.VMEM(residual.shape, jnp.bfloat16), pltpu.SemaphoreType.DMA((2,))],
        n_any=3,
    )
    other_queries = y_flip(queries)
    other_head = core_flip(head_weight)
    own_sum, own_lse, other_sum = call(
        functools.partial(attend_kernel, Z, heads_local, kv_local),
        "attend",
        (
            jax.ShapeDtypeStruct((CAP, q_width), jnp.float32),
            jax.ShapeDtypeStruct((CAP, LANES), jnp.float32),
            jax.ShapeDtypeStruct((CAP, q_width + LANES), jnp.bfloat16),
        ),
        1,
        (scalars(seq_index, partner, *sources), slot_blocks, queries, other_queries, keys_here, values_here, *pieces),
        16,
    )
    got_sum = y_flip(other_sum)
    mine, theirs = call(
        functools.partial(project_kernel, heads_local),
        "project",
        (jax.ShapeDtypeStruct((HALF, width), jnp.float32), jax.ShapeDtypeStruct((HALF, width), jnp.bfloat16)),
        1,
        (scalars(c), own_sum, own_lse, got_sum, staged_out),
        16,
    )

    all_slot = jnp.cumsum(all_mask, axis=1) - 1
    slot_hit = (all_mask[:, None, :] == 1) & (all_slot[:, None, :] == jnp.arange(CAP)[None, :, None])
    slot_targets = jnp.sum(jnp.where(slot_hit, targets.reshape(S, 1, tok_rows), 0), axis=2)
    my_mask = lax.dynamic_slice_in_dim(mask_flags, first_row, tok_rows)
    my_slot = jnp.cumsum(my_mask) - 1
    chosen = (my_mask[None, :] == 1) & (my_slot[None, :] == jnp.arange(CAP)[:, None])

    mine = mine + core_flip(theirs).astype(jnp.float32)
    sent = mine.astype(jnp.bfloat16)
    summed = mine
    for k in range(1, X):
        summed = summed + x_shift(sent, k).astype(jnp.float32)
    hidden = lax.dynamic_slice_in_dim(residual_sel, c * HALF, HALF).astype(jnp.float32) + summed
    squares = jnp.sum(hidden * hidden, axis=1, keepdims=True)
    normed = (hidden * lax.rsqrt(squares / D + norm_eps) * norm_gain[None, :]).astype(jnp.bfloat16)

    own = lax.dynamic_slice_in_dim(normed, x * share, share, 1)
    slabs = [own] + [z_swap(own, k) for k in range(1, Z)]
    n_rows = Y * Z * HALF
    mixed = X == Y
    groups = [g for g in (list(range(min(2, Z))), list(range(2, Z))) if g]
    rows, src_s = [], []
    for group in groups:
        n = len(group) * HALF
        column = jnp.stack([slabs[k] for k in group])
        if mixed:
            step1 = mixed_flip(column, True)
            step2 = mixed_flip(jnp.stack([column, step1]), False)
            rows += [column.reshape(n, share), step1.reshape(n, share), step2.reshape(Y * n, share)]
        else:
            pair = jnp.stack([column, y_flip(column)])
            rows += [pair.reshape(Y * n, share)] + [x_shift(pair, k).reshape(Y * n, share) for k in range(1, X)]
        src_z = jnp.stack([from_z(k) for k in group])
        src_s.append((src_z[None, :] * Y + jnp.stack([y, 1 - y])[:, None]).reshape(-1))
    src_s = jnp.concatenate(src_s)
    from_s = src_s[None, :] == jnp.arange(S)[:, None]
    half_targets = lax.dynamic_slice_in_dim(slot_targets, c * HALF, HALF, 1)
    row_targets = jnp.sum(jnp.where(from_s[:, :, None], half_targets[:, None, :], 0), axis=0).reshape(1, n_rows)
    first = (seq_index * V + x * C) * vocab_rows
    staged = call(
        stage_head_kernel,
        "stage_head",
        (jax.ShapeDtypeStruct(head_weight.shape, jnp.bfloat16),) * 2,
        0,
        (head_weight, other_head, own),
        50,
        scratch=[pltpu.SemaphoreType.DMA((2,))],
        n_any=3,
    )
    send = call(
        functools.partial(logits_kernel, mixed, X, Y, [len(g) for g in groups], V),
        "logits",
        jax.ShapeDtypeStruct((S * V, 1, LANES), jnp.float32),
        1,
        (
            jnp.concatenate([scalars(x, c, first + c * vocab_rows, first + (1 - c) * vocab_rows), src_s.astype(jnp.int32)]),
            row_targets,
            *rows,
            *staged,
        ),
        24,
        4 * n_rows * width * vocab_rows,
        [pltpu.VMEM((n_rows, share), jnp.bfloat16)] * X,
    ).reshape(S * V, LANES)
    got = lax.all_to_all(send, ("seq", "vocab"), 0, 0, tiled=True).reshape(S * X, C, LANES)
    lse = got[:, :, :HALF]
    picked = jnp.sum(got[:, :, HALF : 2 * HALF], axis=0).reshape(CAP)
    best = jnp.max(lse, axis=0)
    nll = (best + jnp.log(jnp.sum(jnp.exp(lse - best[None]), axis=0))).reshape(CAP) - picked
    token_nll = jnp.sum(jnp.where(chosen, nll[:, None], 0.0), axis=0)
    my_levels = lax.dynamic_slice_in_dim(levels, seq_index * (tok_rows // BLOCK), tok_rows // BLOCK)
    token_level = jnp.repeat(my_levels, BLOCK)
    return token_nll / (token_level + 1).astype(jnp.float32)


def solution(mesh):
    in_specs = (
        P("seq", "vocab"),
        P("seq", "vocab"),
        P("seq", "vocab"),
        P("seq", "vocab"),
        P("seq", "vocab"),
        P("vocab", None),
        P("seq", None),
        P(),
        P(("seq", "vocab"), None),
        P(),
        P(),
        P(),
    )
    return jax.shard_map(shards, mesh=mesh, in_specs=in_specs, out_specs=P("seq"), check_vma=False)
```

```python
import functools

import jax
import jax.numpy as jnp
from jax import lax
from jax.experimental import pallas as pl
from jax.experimental.pallas import tpu as pltpu
from jax.sharding import PartitionSpec as P


D = 4096
HEAD_DIM = 128
BLOCK = 32
CAP = 48
HALF = CAP // 2
LANES = 128
SHIFT = BLOCK.bit_length() - 1
C = 2
Y = 2

very_low = -1e30
norm_eps = 1e-06

VMEM = pl.BlockSpec(memory_space=pltpu.VMEM)
SMEM = pl.BlockSpec(memory_space=pltpu.SMEM)
ANY = pl.BlockSpec(memory_space=pl.ANY)
NT = (((1,), (1,)), ((), ()))
MIB = 1 << 20


def call(kernel, outs, args, mib, flops=0, scratch=(), specs=None, out_specs=None):
    n_bytes = sum(a.size * a.dtype.itemsize for a in args)
    return pl.pallas_call(
        kernel,
        out_shape=outs,
        in_specs=specs or [VMEM] * len(args),
        out_specs=out_specs or jax.tree.map(lambda _: VMEM, outs),
        scratch_shapes=list(scratch),
        compiler_params=pltpu.CompilerParams(vmem_limit_bytes=mib * MIB),
        cost_estimate=pl.CostEstimate(flops=flops, bytes_accessed=n_bytes, transcendentals=0),
    )(*args)


def place():
    s, v = lax.axis_index("seq"), lax.axis_index("vocab")
    return s, lax.div(s, Y), lax.rem(s, Y), v, lax.div(v, C), lax.rem(v, C)


def swap_z(z, k, Z):
    return jnp.bitwise_xor(z, k) if Z & (Z - 1) == 0 else lax.rem(z + (Z - k), Z)


def slots_of(row):
    tok = row.shape[1]
    upto = lax.broadcasted_iota(jnp.int32, (tok, tok), 0) <= lax.broadcasted_iota(jnp.int32, (tok, tok), 1)
    row = row.astype(jnp.float32)
    count = jnp.dot(jnp.broadcast_to(row, (8, tok)), upto.astype(jnp.float32), preferred_element_type=jnp.float32)[0:1]
    slots = lax.broadcasted_iota(jnp.int32, (CAP, tok), 0).astype(jnp.float32)
    return ((count - 1.0) == slots) & (row == 1.0)


def exact_dot(a, b, dims):
    return lax.dot_general(a, b, dims, precision=lax.Precision.HIGHEST, preferred_element_type=jnp.float32)


def select_kernel(mask_ref, q_ref, q_out, blk_out):
    s, _, y, _, _, _ = place()
    tok = mask_ref.shape[1]
    block = lax.shift_right_logical(lax.broadcasted_iota(jnp.int32, (CAP, tok), 1), SHIFT).astype(jnp.float32)
    for which in range(2):
        pick = jnp.where(slots_of(mask_ref[pl.ds(s if which == 0 else s + 1 - 2 * y, 1), :]), 1.0, 0.0)
        blk_out[which] = jnp.broadcast_to(jnp.sum(pick * block, axis=1, keepdims=True), (CAP, LANES))
        if which == 0:
            pick = pick.astype(jnp.bfloat16)
            q_out[...] = jnp.dot(pick, q_ref[...], preferred_element_type=jnp.float32).astype(jnp.bfloat16)


def residual_kernel(Z, mask_ref, target_ref, res_ref, after_ref, res_out, target_out):
    s, z, y, _, _, c = place()
    pick = jnp.where(slots_of(mask_ref[pl.ds(s, 1), :]), 1.0, 0.0).astype(jnp.bfloat16)
    res_out[...] = jnp.dot(pick, res_ref[...], preferred_element_type=jnp.float32).astype(jnp.bfloat16)
    wide = target_out.shape[1]
    lane = lax.broadcasted_iota(jnp.int32, (8, wide), 1)
    found = jnp.zeros((8, wide), jnp.float32)
    for p, (k, other) in enumerate(row_order(Z)):
        src = swap_z(z, k, Z) * Y + (1 - y if other else y)
        hit = jnp.where(slots_of(mask_ref[pl.ds(src, 1), :]), 1.0, 0.0)
        half = jnp.where(c == 0, hit[:HALF], hit[HALF:])
        hit = jnp.concatenate([half, jnp.zeros((LANES - HALF, half.shape[1]), jnp.float32)], axis=0)
        row = jnp.broadcast_to(target_ref[pl.ds(src, 1), :].astype(jnp.float32), (8, target_ref.shape[1]))
        ids = exact_dot(row, hit, NT)
        ids = jnp.concatenate([ids] + [jnp.zeros((8, LANES), jnp.float32)] * (wide // LANES - 1), axis=1)
        ids = pltpu.roll(ids, p * HALF, 1) if p else ids
        found = jnp.where((lane >= p * HALF) & (lane < (p + 1) * HALF), ids, found)
    target_out[...] = found.astype(jnp.int32)


def stage_kernel(n, after, *refs):
    sems = refs[-1]
    copies = [pltpu.make_async_copy(refs[i], refs[n + i], sems.at[i]) for i in range(n)]
    for copy in copies:
        copy.start()
    for copy in copies:
        copy.wait()


def stage(after, *arrays):
    n = len(arrays)
    return call(
        functools.partial(stage_kernel, n),
        tuple(jax.ShapeDtypeStruct(a.shape, a.dtype) for a in arrays),
        (after, *arrays),
        1,
        scratch=[pltpu.SemaphoreType.DMA((n,))],
        specs=[ANY] * (n + 1),
        out_specs=(ANY,) * n,
    )


def split3(value):
    high = value.astype(jnp.bfloat16).astype(jnp.float32)
    rest = value - high
    mid = rest.astype(jnp.bfloat16).astype(jnp.float32)
    return high, mid, rest - mid


def attend_kernel(n_pieces, heads, kv_heads, S, blk_ref, q_own, q_other, kn_ref, vn_ref, *refs):
    s, z, y, _, _, _ = place()
    pieces, (own_out, own_lse, other_out) = refs[:n_pieces], refs[n_pieces:]
    group = heads // kv_heads
    tok = kn_ref.shape[0]
    per_dev = tok // BLOCK
    scale = HEAD_DIM ** (-0.5)
    lane = lax.broadcasted_iota(jnp.int32, (CAP, LANES), 1)
    key_block = lax.shift_right_logical(lax.broadcasted_iota(jnp.int32, (CAP, tok), 1), SHIFT)
    for which in range(2):
        q_ref = (q_own, q_other)[which]
        slot_block = blk_ref[which][:, :1].astype(jnp.int32)
        row_block = slot_block + (s if which == 0 else s + 1 - 2 * y) * per_dev
        bias = []
        for k in range(n_pieces):
            source = jnp.where(z >= k, s - k * Y, S)
            seen = (key_block + source * per_dev) < row_block
            bias.append(jnp.concatenate([jnp.where(seen, 0.0, very_low)] * group, axis=0))
        if which == 0:
            bias.append(jnp.concatenate([jnp.where(key_block == slot_block, 0.0, very_low)] * group, axis=0))
        lse_all = jnp.zeros((CAP, LANES), jnp.float32)
        for g in range(kv_heads):
            cols = slice(g * HEAD_DIM, (g + 1) * HEAD_DIM)
            q_g = jnp.concatenate(
                [q_ref[:, (g * group + h) * HEAD_DIM : (g * group + h + 1) * HEAD_DIM] for h in range(group)], axis=0
            )
            keys = [p[0][:, cols] for p in pieces]
            values = [p[1][:, cols] for p in pieces]
            if which == 0:
                keys.append(kn_ref[:, cols])
                values.append(vn_ref[:, cols])
            scores = [
                lax.dot_general(q_g, k, NT, preferred_element_type=jnp.float32) * scale + b for k, b in zip(keys, bias)
            ]
            top = jnp.max(functools.reduce(jnp.maximum, scores), axis=1, keepdims=True)
            weights = [jnp.exp(score - top) for score in scores]
            total = jnp.sum(functools.reduce(jnp.add, weights), axis=1, keepdims=True)
            mixed = functools.reduce(
                jnp.add,
                [jnp.dot(w.astype(jnp.bfloat16), v, preferred_element_type=jnp.float32) for w, v in zip(weights, values)],
            )
            mixed = mixed / total
            lse = top + jnp.log(total)
            for h in range(group):
                head = g * group + h
                rows = slice(h * CAP, (h + 1) * CAP)
                at = slice(head * HEAD_DIM, (head + 1) * HEAD_DIM)
                lse_all = jnp.where(lane == head, lse[rows], lse_all)
                if which == 0:
                    own_out[:, at] = mixed[rows]
                else:
                    other_out[:, at] = mixed[rows].astype(jnp.bfloat16)
        if which == 0:
            own_lse[...] = lse_all
        else:
            high, mid, low = split3(lse_all)
            packed = high + pltpu.roll(mid, 32, 1) + pltpu.roll(low, 64, 1)
            other_out[:, heads * HEAD_DIM :] = packed.astype(jnp.bfloat16)


def project_kernel(heads, own_ref, lse_ref, got_ref, w_ref, mine_out, theirs_out):
    _, _, _, _, _, c = place()
    packed = got_ref[:, heads * HEAD_DIM :].astype(jnp.float32)
    got_lse = packed + pltpu.roll(packed, LANES - 32, 1) + pltpu.roll(packed, LANES - 64, 1)
    own_lse = lse_ref[...]
    top = jnp.maximum(own_lse, got_lse)
    w_own, w_got = jnp.exp(own_lse - top), jnp.exp(got_lse - top)
    total = w_own + w_got
    w_own, w_got = w_own / total, w_got / total
    parts = []
    for h in range(heads):
        at = slice(h * HEAD_DIM, (h + 1) * HEAD_DIM)
        joined = own_ref[:, at] * w_own[:, h : h + 1] + got_ref[:, at].astype(jnp.float32) * w_got[:, h : h + 1]
        parts.append(joined.astype(jnp.bfloat16))
    attention = jnp.concatenate(parts, axis=1)
    first = c == 0
    width = w_ref.shape[1]
    step = min(1024, width)
    for j in range(0, width, step):
        out = jnp.dot(attention, w_ref[:, j : j + step], preferred_element_type=jnp.float32)
        upper, lower = out[:HALF], out[HALF:]
        mine_out[:, j : j + step] = jnp.where(first, upper, lower)
        theirs_out[:, j : j + step] = jnp.where(first, lower, upper).astype(jnp.bfloat16)


def norm_kernel(share, mine_ref, res_ref, gain_ref, *refs):
    _, _, _, _, x, c = place()
    *got, own_out, normed = refs
    res = res_ref[...].astype(jnp.float32)
    hidden = mine_ref[...]
    for ref in got:
        hidden = hidden + ref[...].astype(jnp.float32)
    hidden = jnp.where(c == 0, res[:HALF], res[HALF:]) + hidden
    squares = jnp.sum(hidden * hidden, axis=1, keepdims=True)
    normed[...] = hidden * lax.rsqrt(squares / D + norm_eps) * gain_ref[...]
    own_out[...] = normed[:, pl.ds(pl.multiple_of(x * share, LANES), share)].astype(jnp.bfloat16)


def row_groups(Z):
    return [g for g in (list(range(min(2, Z))), list(range(2, Z))) if g]


def row_order(Z):
    return [(k, other) for group in row_groups(Z) for other in (False, True) for k in group]


def logits_kernel(mixed, X, Z, V, target_ref, *refs):
    s, z, y, v, x, c = place()
    share = refs[0].shape[1]
    sizes = [len(g) for g in row_groups(Z)]
    n_rows = Y * Z * HALF
    n_refs = (3 if mixed else X) * len(sizes)
    pieces, (w_own, w_other, out_ref, *rows) = refs[:n_refs], refs[n_refs:]
    base = 0
    for i, size in enumerate(sizes):
        n = size * HALF
        if mixed:
            column, step1, step2 = pieces[3 * i : 3 * i + 3]
            near, far = rows
            near[base : base + n] = column[...]
            far[base + n : base + 2 * n] = step2[n:]

            @pl.when(c == 0)
            def _(base=base, n=n, step1=step1, step2=step2):
                near[base + n : base + 2 * n] = step2[:n]
                far[base : base + n] = step1[...]

            @pl.when(c != 0)
            def _(base=base, n=n, step1=step1, step2=step2):
                near[base + n : base + 2 * n] = step1[...]
                far[base : base + n] = step2[:n]
        else:
            for k in range(X):
                rows[k][base : base + Y * n] = pieces[X * i + k][...]
        base += Y * n
    logits = []
    for w in (w_own, w_other):
        total = None
        for k in range(X):
            at = pl.multiple_of(lax.rem(x + (X - k), X) * share, LANES)
            part = lax.dot_general(w[:, pl.ds(at, share)], rows[k][...], NT, preferred_element_type=jnp.float32)
            total = part if total is None else total + part
        logits.append(total)
    vocab_rows = w_own.shape[0]
    starts = [(s * V + v) * vocab_rows, (s * V + v + 1 - 2 * c) * vocab_rows]
    top = jnp.maximum(jnp.max(logits[0], axis=0, keepdims=True), jnp.max(logits[1], axis=0, keepdims=True))
    summed = 0.0
    picked = 0.0
    wanted = target_ref[0:1, :n_rows]
    for start, lg in zip(starts, logits):
        ids = lax.broadcasted_iota(jnp.int32, lg.shape, 0)
        summed = summed + jnp.sum(jnp.exp(lg - top), axis=0, keepdims=True)
        picked = picked + jnp.sum(jnp.where(ids == wanted - start, lg, 0.0), axis=0, keepdims=True)
    lse = top + jnp.log(summed)
    wide = target_ref.shape[1]
    pad = [jnp.zeros((1, wide - n_rows), jnp.float32)] if wide > n_rows else []
    lse = jnp.broadcast_to(jnp.concatenate([lse, *pad], axis=1), (8, wide))
    picked = jnp.broadcast_to(jnp.concatenate([picked, *pad], axis=1), (8, wide))
    lane = lax.broadcasted_iota(jnp.int32, (8, LANES), 1)
    for p, (k, other) in enumerate(row_order(Z)):
        a = pltpu.roll(lse, (wide - p * HALF) % wide, 1)[:, :LANES]
        b = pltpu.roll(picked, (wide - p * HALF + HALF) % wide, 1)[:, :LANES]
        row = jnp.where(lane < HALF, a, b)[0:1]
        first = (swap_z(z, k, Z) * Y + (1 - y if other else y)) * V
        for i in range(V):
            out_ref[first + i] = row


def loss_kernel(levels_ref, mask_ref, got_ref, out_ref):
    s, _, _, _, _, _ = place()
    got = got_ref[...]
    tok = mask_ref.shape[1]
    core = lax.rem(lax.broadcasted_iota(jnp.int32, got.shape, 0), C)
    lane = lax.broadcasted_iota(jnp.int32, (8, LANES), 1)
    nll = jnp.zeros((8, LANES), jnp.float32)
    for half in range(C):
        here = core == half
        best = jnp.max(jnp.where(here, got, -jnp.inf), axis=0, keepdims=True)
        total = jnp.sum(jnp.where(here, jnp.exp(got - best), 0.0), axis=0, keepdims=True)
        picked = jnp.broadcast_to(jnp.sum(jnp.where(here, got, 0.0), axis=0, keepdims=True), (8, LANES))
        value = best + jnp.log(total) - pltpu.roll(picked, LANES - HALF, 1)
        value = pltpu.roll(value, half * HALF, 1) if half else value
        nll = jnp.where((lane >= half * HALF) & (lane < (half + 1) * HALF), value, nll)
    chosen = jnp.where(slots_of(mask_ref[pl.ds(s, 1), :]), 1.0, 0.0)
    chosen = jnp.concatenate([chosen, jnp.zeros((LANES - CAP, tok), jnp.float32)], axis=0)
    token_nll = exact_dot(nll, chosen, (((1,), (0,)), ((), ())))[0:1]
    block = lax.shift_right_logical(lax.broadcasted_iota(jnp.int32, (1, tok), 1), SHIFT)
    weight = jnp.ones((1, tok), jnp.float32)
    for b in range(tok // BLOCK):
        weight = jnp.where(block == b, (levels_ref[s * (tok // BLOCK) + b] + 1).astype(jnp.float32), weight)
    out_ref[...] = token_nll / weight


def shards(
    q_noised,
    key_clean,
    value_clean,
    key_noised,
    value_noised,
    out_weight,
    residual,
    norm_gain,
    head_weight,
    targets,
    mask_flags,
    levels,
):
    tok_rows, q_width = q_noised.shape
    width = residual.shape[1]
    heads_local = q_width // HEAD_DIM
    kv_local = key_clean.shape[1] // HEAD_DIM
    vocab_rows = head_weight.shape[0]
    S = lax.axis_size("seq")
    V = lax.axis_size("vocab")
    X = V // C
    Z = S // Y
    share = width // X
    every = [(zi, yi, xi, ci) for zi in range(Z) for yi in range(Y) for xi in range(X) for ci in range(C)]

    def permute(block, to):
        def dev(zi, yi, xi, ci):
            return ((zi * Y + yi) * X + xi) * C + ci

        return lax.ppermute(block, ("seq", "vocab"), [(dev(*e), dev(*to(*e))) for e in every if to(*e)[0] < Z])

    def core_flip(block):
        return permute(block, lambda a, b, e, f: (a, b, e, 1 - f))

    def x_shift(block, k):
        return permute(block, lambda a, b, e, f: (a, b, (e + k) % X, f))

    def y_flip(block):
        return permute(block, lambda a, b, e, f: (a, 1 - b, e, f))

    def z_up(block, k):
        return permute(block, lambda a, b, e, f: (a + k, b, e, f))

    def z_swap(block, k):
        paired = Z & (Z - 1) == 0
        return permute(block, lambda a, b, e, f: (a ^ k if paired else (a + k) % Z, b, e, f))

    def mixed_flip(block, x_core):
        return permute(block, lambda a, b, e, f: (a, b, 1 - e, f) if f == x_core else (a, 1 - b, e, f))

    def struct(*shape, dtype=jnp.bfloat16):
        return jax.ShapeDtypeStruct(shape, dtype)

    all_mask = mask_flags.reshape(S, tok_rows)
    own_kv = jnp.stack([key_clean, value_clean])
    pieces = [own_kv] + [z_up(own_kv, k) for k in range(1, Z)]
    queries, slot_blocks = call(
        select_kernel, (struct(CAP, q_width), struct(2, CAP, LANES, dtype=jnp.float32)), (all_mask, q_noised), 8
    )
    other_queries = y_flip(queries)
    other_head = core_flip(head_weight)
    keys_here, values_here, staged_out = stage(queries, key_noised, value_noised, out_weight)
    own_sum, own_lse, other_sum = call(
        functools.partial(attend_kernel, Z, heads_local, kv_local, S),
        (
            struct(CAP, q_width, dtype=jnp.float32),
            struct(CAP, LANES, dtype=jnp.float32),
            struct(CAP, q_width + LANES),
        ),
        (slot_blocks, queries, other_queries, keys_here, values_here, *pieces),
        16,
    )
    got_sum = y_flip(other_sum)
    mine, theirs = call(
        functools.partial(project_kernel, heads_local),
        (struct(HALF, width, dtype=jnp.float32), struct(HALF, width)),
        (own_sum, own_lse, got_sum, staged_out),
        16,
    )

    mine = mine + core_flip(theirs).astype(jnp.float32)
    sent = mine.astype(jnp.bfloat16)
    n_rows = Y * Z * HALF
    wide = -(-n_rows // LANES) * LANES
    residual_sel, row_targets = call(
        functools.partial(residual_kernel, Z),
        (struct(CAP, width), struct(8, wide, dtype=jnp.int32)),
        (all_mask, targets.reshape(S, tok_rows), residual, theirs),
        8,
    )
    own = call(
        functools.partial(norm_kernel, share),
        struct(HALF, share),
        (mine, residual_sel, norm_gain.reshape(1, width), *[x_shift(sent, k) for k in range(1, X)]),
        8,
        scratch=[pltpu.VMEM((HALF, width), jnp.float32)],
    )

    slabs = [own]
    for k in range(1, Z):
        slabs.append(z_swap(own, k))
    mixed = X == Y
    rows = []
    for group in row_groups(Z):
        n = len(group) * HALF
        column = jnp.stack([slabs[k] for k in group])
        if mixed:
            step1 = mixed_flip(column, 0)
            both = jnp.stack([column, step1])
            step2 = mixed_flip(both, 1)
            rows += [column.reshape(n, share), step1.reshape(n, share), step2.reshape(Y * n, share)]
        else:
            pair = jnp.stack([column, y_flip(column)])
            rows += [pair.reshape(Y * n, share)] + [x_shift(pair, k).reshape(Y * n, share) for k in range(1, X)]
    staged = stage(own, head_weight, other_head)
    send = call(
        functools.partial(logits_kernel, mixed, X, Z, V),
        struct(S * V, 1, LANES, dtype=jnp.float32),
        (row_targets, *rows, *staged),
        24,
        4 * n_rows * width * vocab_rows,
        [pltpu.VMEM((n_rows, share), jnp.bfloat16)] * X,
    ).reshape(S * V, LANES)
    got = lax.all_to_all(send, ("seq", "vocab"), 0, 0, tiled=True)
    loss = call(
        loss_kernel, struct(1, tok_rows, dtype=jnp.float32), (levels, all_mask, got), 4, specs=[SMEM, VMEM, VMEM]
    )
    return loss.reshape(tok_rows)


def solution(mesh):
    in_specs = (
        P("seq", "vocab"),
        P("seq", "vocab"),
        P("seq", "vocab"),
        P("seq", "vocab"),
        P("seq", "vocab"),
        P("vocab", None),
        P("seq", None),
        P(),
        P(("seq", "vocab"), None),
        P(),
        P(),
        P(),
    )
    return jax.shard_map(shards, mesh=mesh, in_specs=in_specs, out_specs=P("seq"), check_vma=False)
```

```python
import functools

import jax
import jax.numpy as jnp
from jax import lax
from jax.experimental import pallas as pl
from jax.experimental.pallas import tpu as pltpu
from jax.sharding import PartitionSpec as P


D = 4096
HEAD_DIM = 128
BLOCK = 32
CAP = 48
HALF = CAP // 2
LANES = 128
SHIFT = BLOCK.bit_length() - 1
C = 2
Y = 2

very_low = -1e30
norm_eps = 1e-06

VMEM = pl.BlockSpec(memory_space=pltpu.VMEM)
SMEM = pl.BlockSpec(memory_space=pltpu.SMEM)
ANY = pl.BlockSpec(memory_space=pl.ANY)
NT = (((1,), (1,)), ((), ()))
MIB = 1 << 20


def call(kernel, outs, args, mib, flops=0, scratch=(), specs=None, out_specs=None):
    n_bytes = sum(a.size * a.dtype.itemsize for a in args)
    return pl.pallas_call(
        kernel,
        out_shape=outs,
        in_specs=specs or [VMEM] * len(args),
        out_specs=out_specs or jax.tree.map(lambda _: VMEM, outs),
        scratch_shapes=list(scratch),
        compiler_params=pltpu.CompilerParams(vmem_limit_bytes=mib * MIB),
        cost_estimate=pl.CostEstimate(flops=flops, bytes_accessed=n_bytes, transcendentals=0),
    )(*args)


def place():
    s, v = lax.axis_index("seq"), lax.axis_index("vocab")
    return s, lax.div(s, Y), lax.rem(s, Y), v, lax.div(v, C), lax.rem(v, C)


def swap_z(z, k, Z):
    return jnp.bitwise_xor(z, k) if Z & (Z - 1) == 0 else lax.rem(z + (Z - k), Z)


def slots_of(row):
    tok = row.shape[1]
    upto = lax.broadcasted_iota(jnp.int32, (tok, tok), 0) <= lax.broadcasted_iota(jnp.int32, (tok, tok), 1)
    row = row.astype(jnp.float32)
    count = jnp.dot(jnp.broadcast_to(row, (8, tok)), upto.astype(jnp.float32), preferred_element_type=jnp.float32)[0:1]
    slots = lax.broadcasted_iota(jnp.int32, (CAP, tok), 0).astype(jnp.float32)
    return ((count - 1.0) == slots) & (row == 1.0)


def exact_dot(a, b, dims):
    return lax.dot_general(a, b, dims, precision=lax.Precision.HIGHEST, preferred_element_type=jnp.float32)


def select_kernel(mask_ref, q_ref, q_out, blk_out):
    s, _, y, _, _, _ = place()
    tok = mask_ref.shape[1]
    block = lax.shift_right_logical(lax.broadcasted_iota(jnp.int32, (CAP, tok), 1), SHIFT).astype(jnp.float32)
    for which in range(2):
        pick = jnp.where(slots_of(mask_ref[pl.ds(s if which == 0 else s + 1 - 2 * y, 1), :]), 1.0, 0.0)
        blk_out[which] = jnp.broadcast_to(jnp.sum(pick * block, axis=1, keepdims=True), (CAP, LANES))
        if which == 0:
            pick = pick.astype(jnp.bfloat16)
            q_out[...] = jnp.dot(pick, q_ref[...], preferred_element_type=jnp.float32).astype(jnp.bfloat16)


def residual_kernel(Z, levels_ref, mask_ref, target_ref, res_ref, after_ref, res_out, target_out, chosen_out, weight_out):
    s, z, y, _, _, c = place()
    pick = jnp.where(slots_of(mask_ref[pl.ds(s, 1), :]), 1.0, 0.0)
    tok = pick.shape[1]
    chosen_out[...] = jnp.concatenate([pick, jnp.zeros((LANES - CAP, tok), jnp.float32)], axis=0)
    block = lax.shift_right_logical(lax.broadcasted_iota(jnp.int32, (8, tok), 1), SHIFT)
    weight = jnp.ones((8, tok), jnp.float32)
    for b in range(tok // BLOCK):
        weight = jnp.where(block == b, (levels_ref[s * (tok // BLOCK) + b] + 1).astype(jnp.float32), weight)
    weight_out[...] = weight
    pick = pick.astype(jnp.bfloat16)
    res_out[...] = jnp.dot(pick, res_ref[...], preferred_element_type=jnp.float32).astype(jnp.bfloat16)
    wide = target_out.shape[1]
    lane = lax.broadcasted_iota(jnp.int32, (8, wide), 1)
    found = jnp.zeros((8, wide), jnp.float32)
    for p, (k, other) in enumerate(row_order(Z)):
        src = swap_z(z, k, Z) * Y + (1 - y if other else y)
        hit = jnp.where(slots_of(mask_ref[pl.ds(src, 1), :]), 1.0, 0.0)
        half = jnp.where(c == 0, hit[:HALF], hit[HALF:])
        hit = jnp.concatenate([half, jnp.zeros((LANES - HALF, half.shape[1]), jnp.float32)], axis=0)
        row = jnp.broadcast_to(target_ref[pl.ds(src, 1), :].astype(jnp.float32), (8, target_ref.shape[1]))
        ids = exact_dot(row, hit, NT)
        ids = jnp.concatenate([ids] + [jnp.zeros((8, LANES), jnp.float32)] * (wide // LANES - 1), axis=1)
        ids = pltpu.roll(ids, p * HALF, 1) if p else ids
        found = jnp.where((lane >= p * HALF) & (lane < (p + 1) * HALF), ids, found)
    target_out[...] = found.astype(jnp.int32)


def stage_kernel(n, after, *refs):
    sems = refs[-1]
    copies = [pltpu.make_async_copy(refs[i], refs[n + i], sems.at[i]) for i in range(n)]
    for copy in copies:
        copy.start()
    for copy in copies:
        copy.wait()


def stage(after, *arrays):
    n = len(arrays)
    return call(
        functools.partial(stage_kernel, n),
        tuple(jax.ShapeDtypeStruct(a.shape, a.dtype) for a in arrays),
        (after, *arrays),
        1,
        scratch=[pltpu.SemaphoreType.DMA((n,))],
        specs=[ANY] * (n + 1),
        out_specs=(ANY,) * n,
    )


def split3(value):
    high = value.astype(jnp.bfloat16).astype(jnp.float32)
    rest = value - high
    mid = rest.astype(jnp.bfloat16).astype(jnp.float32)
    return high, mid, rest - mid


def attend_kernel(Z, heads, kv_heads, S, blk_ref, q_own, q_other, kn_ref, vn_ref, *refs):
    s, z, y, _, _, _ = place()
    *pieces, own_out, own_lse, other_out = refs
    passed = pieces.pop() if Z == 4 else None

    def piece(k, part, cols):
        block = pieces[k][part][:, cols]
        return block if passed is None or k != 2 else jnp.where(z == Z - 1, passed[part][:, cols], block)

    group = heads // kv_heads
    tok = kn_ref.shape[0]
    per_dev = tok // BLOCK
    scale = HEAD_DIM ** (-0.5)
    lane = lax.broadcasted_iota(jnp.int32, (CAP, LANES), 1)
    key_block = lax.shift_right_logical(lax.broadcasted_iota(jnp.int32, (CAP, tok), 1), SHIFT)
    for which in range(2):
        q_ref = (q_own, q_other)[which]
        slot_block = blk_ref[which][:, :1].astype(jnp.int32)
        row_block = slot_block + (s if which == 0 else s + 1 - 2 * y) * per_dev
        bias = []
        for k in range(Z):
            source = jnp.where(z >= k, s - k * Y, S)
            seen = (key_block + source * per_dev) < row_block
            bias.append(jnp.concatenate([jnp.where(seen, 0.0, very_low)] * group, axis=0))
        if which == 0:
            bias.append(jnp.concatenate([jnp.where(key_block == slot_block, 0.0, very_low)] * group, axis=0))
        lse_all = jnp.zeros((CAP, LANES), jnp.float32)
        for g in range(kv_heads):
            cols = slice(g * HEAD_DIM, (g + 1) * HEAD_DIM)
            q_g = jnp.concatenate(
                [q_ref[:, (g * group + h) * HEAD_DIM : (g * group + h + 1) * HEAD_DIM] for h in range(group)], axis=0
            )
            keys = [piece(k, 0, cols) for k in range(Z)]
            values = [piece(k, 1, cols) for k in range(Z)]
            if which == 0:
                keys.append(kn_ref[:, cols])
                values.append(vn_ref[:, cols])
            scores = [
                lax.dot_general(q_g, k, NT, preferred_element_type=jnp.float32) * scale + b for k, b in zip(keys, bias)
            ]
            top = jnp.max(functools.reduce(jnp.maximum, scores), axis=1, keepdims=True)
            weights = [jnp.exp(score - top) for score in scores]
            total = jnp.sum(functools.reduce(jnp.add, weights), axis=1, keepdims=True)
            mixed = functools.reduce(
                jnp.add,
                [jnp.dot(w.astype(jnp.bfloat16), v, preferred_element_type=jnp.float32) for w, v in zip(weights, values)],
            )
            mixed = mixed / total
            lse = top + jnp.log(total)
            for h in range(group):
                head = g * group + h
                rows = slice(h * CAP, (h + 1) * CAP)
                at = slice(head * HEAD_DIM, (head + 1) * HEAD_DIM)
                lse_all = jnp.where(lane == head, lse[rows], lse_all)
                if which == 0:
                    own_out[:, at] = mixed[rows]
                else:
                    other_out[:, at] = mixed[rows].astype(jnp.bfloat16)
        if which == 0:
            own_lse[...] = lse_all
        else:
            high, mid, low = split3(lse_all)
            packed = high + pltpu.roll(mid, 32, 1) + pltpu.roll(low, 64, 1)
            other_out[:, heads * HEAD_DIM :] = packed.astype(jnp.bfloat16)


def project_kernel(heads, own_ref, lse_ref, got_ref, w_ref, mine_out, theirs_out):
    _, _, _, _, _, c = place()
    packed = got_ref[:, heads * HEAD_DIM :].astype(jnp.float32)
    got_lse = packed + pltpu.roll(packed, LANES - 32, 1) + pltpu.roll(packed, LANES - 64, 1)
    own_lse = lse_ref[...]
    top = jnp.maximum(own_lse, got_lse)
    w_own, w_got = jnp.exp(own_lse - top), jnp.exp(got_lse - top)
    total = w_own + w_got
    w_own, w_got = w_own / total, w_got / total
    parts = []
    for h in range(heads):
        at = slice(h * HEAD_DIM, (h + 1) * HEAD_DIM)
        joined = own_ref[:, at] * w_own[:, h : h + 1] + got_ref[:, at].astype(jnp.float32) * w_got[:, h : h + 1]
        parts.append(joined.astype(jnp.bfloat16))
    attention = jnp.concatenate(parts, axis=1)
    first = c == 0
    width = w_ref.shape[1]
    step = min(1024, width)
    for j in range(0, width, step):
        out = jnp.dot(attention, w_ref[:, j : j + step], preferred_element_type=jnp.float32)
        upper, lower = out[:HALF], out[HALF:]
        mine_out[:, j : j + step] = jnp.where(first, upper, lower)
        theirs_out[:, j : j + step] = jnp.where(first, lower, upper).astype(jnp.bfloat16)


def norm_kernel(share, mine_ref, res_ref, gain_ref, *refs):
    _, _, _, _, x, c = place()
    *got, full_out, own_out, normed = refs
    res = res_ref[...].astype(jnp.float32)
    hidden = mine_ref[...]
    for ref in got:
        hidden = hidden + ref[...].astype(jnp.float32)
    hidden = jnp.where(c == 0, res[:HALF], res[HALF:]) + hidden
    squares = jnp.sum(hidden * hidden, axis=1, keepdims=True)
    normed[...] = hidden * lax.rsqrt(squares / D + norm_eps) * gain_ref[...]
    full_out[...] = normed[...].astype(jnp.bfloat16)
    own_out[...] = normed[:, pl.ds(pl.multiple_of(x * share, LANES), share)].astype(jnp.bfloat16)


def row_order(Z):
    return [(0, False), (0, True)] + [(k, other) for other in (False, True) for k in range(1, Z)]


def logits_kernel(mixed, X, Z, V, target_ref, *refs):
    s, z, y, v, x, c = place()
    share = refs[0].shape[1] // X
    n_rows = Y * Z * HALF
    n_refs = 2 + (3 if mixed else X)
    (own, across, *pieces), (w_own, w_other, out_ref, *rows) = refs[:n_refs], refs[n_refs:]
    n = (Z - 1) * HALF
    base = 2 * HALF
    for k in range(X):
        at = pl.multiple_of(lax.rem(x + (X - k), X) * share, LANES)
        rows[k][:HALF] = own[:, pl.ds(at, share)]
        rows[k][HALF:base] = across[:, pl.ds(at, share)]
    if mixed:
        column, step1, step2 = pieces
        near, far = rows
        near[base : base + n] = column[...]
        far[base + n :] = step2[n:]

        @pl.when(c == 0)
        def _():
            near[base + n :] = step2[:n]
            far[base : base + n] = step1[...]

        @pl.when(c != 0)
        def _():
            near[base + n :] = step1[...]
            far[base : base + n] = step2[:n]
    else:
        for k in range(X):
            rows[k][base:] = pieces[k][...]
    logits = []
    for w in (w_own, w_other):
        total = None
        for k in range(X):
            at = pl.multiple_of(lax.rem(x + (X - k), X) * share, LANES)
            part = lax.dot_general(w[:, pl.ds(at, share)], rows[k][...], NT, preferred_element_type=jnp.float32)
            total = part if total is None else total + part
        logits.append(total)
    vocab_rows = w_own.shape[0]
    starts = [(s * V + v) * vocab_rows, (s * V + v + 1 - 2 * c) * vocab_rows]
    top = jnp.maximum(jnp.max(logits[0], axis=0, keepdims=True), jnp.max(logits[1], axis=0, keepdims=True))
    summed = 0.0
    picked = 0.0
    wanted = target_ref[0:1, :n_rows]
    for start, lg in zip(starts, logits):
        ids = lax.broadcasted_iota(jnp.int32, lg.shape, 0)
        summed = summed + jnp.sum(jnp.exp(lg - top), axis=0, keepdims=True)
        picked = picked + jnp.sum(jnp.where(ids == wanted - start, lg, 0.0), axis=0, keepdims=True)
    lse = top + jnp.log(summed)
    wide = target_ref.shape[1]
    pad = [jnp.zeros((1, wide - n_rows), jnp.float32)] if wide > n_rows else []
    lse = jnp.broadcast_to(jnp.concatenate([lse, *pad], axis=1), (8, wide))
    picked = jnp.broadcast_to(jnp.concatenate([picked, *pad], axis=1), (8, wide))
    lane = lax.broadcasted_iota(jnp.int32, (8, LANES), 1)
    for p, (k, other) in enumerate(row_order(Z)):
        a = pltpu.roll(lse, (wide - p * HALF) % wide, 1)[:, :LANES]
        b = pltpu.roll(picked, (wide - p * HALF + HALF) % wide, 1)[:, :LANES]
        row = jnp.where(lane < HALF, a, b)[0:1]
        first = (swap_z(z, k, Z) * Y + (1 - y if other else y)) * V
        for i in range(V):
            out_ref[first + i] = row


def loss_kernel(chosen_ref, weight_ref, got_ref, out_ref):
    got = got_ref[...]
    core = lax.rem(lax.broadcasted_iota(jnp.int32, got.shape, 0), C)
    lane = lax.broadcasted_iota(jnp.int32, (8, LANES), 1)
    nll = jnp.zeros((8, LANES), jnp.float32)
    for half in range(C):
        here = core == half
        best = jnp.max(jnp.where(here, got, -jnp.inf), axis=0, keepdims=True)
        total = jnp.sum(jnp.where(here, jnp.exp(got - best), 0.0), axis=0, keepdims=True)
        picked = jnp.broadcast_to(jnp.sum(jnp.where(here, got, 0.0), axis=0, keepdims=True), (8, LANES))
        value = best + jnp.log(total) - pltpu.roll(picked, LANES - HALF, 1)
        value = pltpu.roll(value, half * HALF, 1) if half else value
        nll = jnp.where((lane >= half * HALF) & (lane < (half + 1) * HALF), value, nll)
    token_nll = exact_dot(nll, chosen_ref[...], (((1,), (0,)), ((), ())))
    out_ref[...] = (token_nll / weight_ref[...])[0:1]


def shards(
    q_noised,
    key_clean,
    value_clean,
    key_noised,
    value_noised,
    out_weight,
    residual,
    norm_gain,
    head_weight,
    targets,
    mask_flags,
    levels,
):
    tok_rows, q_width = q_noised.shape
    width = residual.shape[1]
    heads_local = q_width // HEAD_DIM
    kv_local = key_clean.shape[1] // HEAD_DIM
    vocab_rows = head_weight.shape[0]
    S = lax.axis_size("seq")
    V = lax.axis_size("vocab")
    X = V // C
    Z = S // Y
    share = width // X
    every = [(zi, yi, xi, ci) for zi in range(Z) for yi in range(Y) for xi in range(X) for ci in range(C)]

    def permute(block, to):
        def dev(zi, yi, xi, ci):
            return ((zi * Y + yi) * X + xi) * C + ci

        return lax.ppermute(block, ("seq", "vocab"), [(dev(*e), dev(*to(*e))) for e in every if to(*e)[0] < Z])

    def core_flip(block):
        return permute(block, lambda a, b, e, f: (a, b, e, 1 - f))

    def x_shift(block, k):
        return permute(block, lambda a, b, e, f: (a, b, (e + k) % X, f))

    def y_flip(block):
        return permute(block, lambda a, b, e, f: (a, 1 - b, e, f))

    def z_up(block, k):
        return permute(block, lambda a, b, e, f: (a + k, b, e, f))

    def along_z(block, pairs):
        return permute(block, lambda a, b, e, f: (dict(pairs).get(a, Z), b, e, f))

    def z_swap(block, k):
        paired = Z & (Z - 1) == 0
        return permute(block, lambda a, b, e, f: (a ^ k if paired else (a + k) % Z, b, e, f))

    def mixed_flip(block, x_core):
        return permute(block, lambda a, b, e, f: (a, b, 1 - e, f) if f == x_core else (a, 1 - b, e, f))

    def struct(*shape, dtype=jnp.bfloat16):
        return jax.ShapeDtypeStruct(shape, dtype)

    all_mask = mask_flags.reshape(S, tok_rows)
    own_kv = jnp.stack([key_clean, value_clean])
    next_kv = z_up(own_kv, 1)
    if Z == 4:
        far_kv = along_z(own_kv, ((0, 3),))
        second_kv = along_z(own_kv, ((0, 2),))
        passed_kv = along_z(next_kv, ((2, 3),))
        pieces = [own_kv, next_kv, second_kv, far_kv, passed_kv]
    else:
        pieces = [own_kv, next_kv] + [z_up(own_kv, k) for k in range(2, Z)]
    queries, slot_blocks = call(
        select_kernel, (struct(CAP, q_width), struct(2, CAP, LANES, dtype=jnp.float32)), (all_mask, q_noised), 8
    )
    other_queries = y_flip(queries)
    other_head = core_flip(head_weight)
    keys_here, values_here = stage(queries, key_noised, value_noised)
    own_sum, own_lse, other_sum = call(
        functools.partial(attend_kernel, Z, heads_local, kv_local, S),
        (
            struct(CAP, q_width, dtype=jnp.float32),
            struct(CAP, LANES, dtype=jnp.float32),
            struct(CAP, q_width + LANES),
        ),
        (slot_blocks, queries, other_queries, keys_here, values_here, *pieces),
        16,
    )
    got_sum = y_flip(other_sum)
    (staged_out,) = stage(other_sum, out_weight)
    mine, theirs = call(
        functools.partial(project_kernel, heads_local),
        (struct(HALF, width, dtype=jnp.float32), struct(HALF, width)),
        (own_sum, own_lse, got_sum, staged_out),
        16,
    )

    mine = mine + core_flip(theirs).astype(jnp.float32)
    sent = mine.astype(jnp.bfloat16)
    n_rows = Y * Z * HALF
    wide = -(-n_rows // LANES) * LANES
    residual_sel, row_targets, chosen, weight = call(
        functools.partial(residual_kernel, Z),
        (
            struct(CAP, width),
            struct(8, wide, dtype=jnp.int32),
            struct(LANES, tok_rows, dtype=jnp.float32),
            struct(8, tok_rows, dtype=jnp.float32),
        ),
        (levels, all_mask, targets.reshape(S, tok_rows), residual, theirs),
        8,
        specs=[SMEM] + [VMEM] * 4,
    )
    own_full, own = call(
        functools.partial(norm_kernel, share),
        (struct(HALF, width), struct(HALF, share)),
        (mine, residual_sel, norm_gain.reshape(1, width), *[x_shift(sent, k) for k in range(1, X)]),
        8,
        scratch=[pltpu.VMEM((HALF, width), jnp.float32)],
    )

    slabs = []
    for k in range(1, Z):
        slabs.append(z_swap(own, k))
    across = y_flip(own_full)
    mixed = X == Y
    n = (Z - 1) * HALF
    column = jnp.stack(slabs)
    if mixed:
        step1 = mixed_flip(column, 0)
        step2 = mixed_flip(jnp.stack([column, step1]), 1)
        rows = [column.reshape(n, share), step1.reshape(n, share), step2.reshape(Y * n, share)]
    else:
        pair = jnp.stack([column, y_flip(column)])
        rows = [pair.reshape(Y * n, share)] + [x_shift(pair, k).reshape(Y * n, share) for k in range(1, X)]
    staged = stage(own, head_weight, other_head)
    send = call(
        functools.partial(logits_kernel, mixed, X, Z, V),
        struct(S * V, 1, LANES, dtype=jnp.float32),
        (row_targets, own_full, across, *rows, *staged),
        24,
        4 * n_rows * width * vocab_rows,
        [pltpu.VMEM((n_rows, share), jnp.bfloat16)] * X,
    ).reshape(S * V, LANES)
    got = lax.all_to_all(send, ("seq", "vocab"), 0, 0, tiled=True)
    loss = call(loss_kernel, struct(1, tok_rows, dtype=jnp.float32), (chosen, weight, got), 4)
    return loss.reshape(tok_rows)


def solution(mesh):
    in_specs = (
        P("seq", "vocab"),
        P("seq", "vocab"),
        P("seq", "vocab"),
        P("seq", "vocab"),
        P("seq", "vocab"),
        P("vocab", None),
        P("seq", None),
        P(),
        P(("seq", "vocab"), None),
        P(),
        P(),
        P(),
    )
    return jax.shard_map(shards, mesh=mesh, in_specs=in_specs, out_specs=P("seq"), check_vma=False)
```

```python
import functools

import jax
import jax.numpy as jnp
from jax import lax
from jax.experimental import pallas as pl
from jax.experimental.pallas import tpu as pltpu
from jax.sharding import PartitionSpec as P


D = 4096
HEAD_DIM = 128
BLOCK = 32
CAP = 48
HALF = CAP // 2
LANES = 128
SHIFT = BLOCK.bit_length() - 1
C = 2
Y = 2

very_low = -1e30
norm_eps = 1e-06

GROUPS = [[1], [3], [2]]
STRAIGHT = [[2]]

VMEM = pl.BlockSpec(memory_space=pltpu.VMEM)
SMEM = pl.BlockSpec(memory_space=pltpu.SMEM)
ANY = pl.BlockSpec(memory_space=pl.ANY)
NT = (((1,), (1,)), ((), ()))
MIB = 1 << 20


def call(kernel, outs, args, mib, flops=0, scratch=(), specs=None, out_specs=None):
    n_bytes = sum(a.size * a.dtype.itemsize for a in args)
    return pl.pallas_call(
        kernel,
        out_shape=outs,
        in_specs=specs or [VMEM] * len(args),
        out_specs=out_specs or jax.tree.map(lambda _: VMEM, outs),
        scratch_shapes=list(scratch),
        compiler_params=pltpu.CompilerParams(vmem_limit_bytes=mib * MIB),
        cost_estimate=pl.CostEstimate(flops=flops, bytes_accessed=n_bytes, transcendentals=0),
    )(*args)


def place():
    s, v = lax.axis_index("seq"), lax.axis_index("vocab")
    return s, lax.div(s, Y), lax.rem(s, Y), v, lax.div(v, C), lax.rem(v, C)


def swap_z(z, k, Z):
    return jnp.bitwise_xor(z, k) if Z & (Z - 1) == 0 else lax.rem(z + (Z - k), Z)


def slots_of(row):
    tok = row.shape[1]
    upto = lax.broadcasted_iota(jnp.int32, (tok, tok), 0) <= lax.broadcasted_iota(jnp.int32, (tok, tok), 1)
    row = row.astype(jnp.float32)
    count = jnp.dot(jnp.broadcast_to(row, (8, tok)), upto.astype(jnp.float32), preferred_element_type=jnp.float32)[0:1]
    slots = lax.broadcasted_iota(jnp.int32, (CAP, tok), 0).astype(jnp.float32)
    return ((count - 1.0) == slots) & (row == 1.0)


def exact_dot(a, b, dims):
    return lax.dot_general(a, b, dims, precision=lax.Precision.HIGHEST, preferred_element_type=jnp.float32)


def select_kernel(mask_ref, q_ref, q_out, blk_out):
    s, _, y, _, _, _ = place()
    tok = mask_ref.shape[1]
    block = lax.shift_right_logical(lax.broadcasted_iota(jnp.int32, (CAP, tok), 1), SHIFT).astype(jnp.float32)
    for which in range(2):
        pick = jnp.where(slots_of(mask_ref[pl.ds(s if which == 0 else s + 1 - 2 * y, 1), :]), 1.0, 0.0)
        blk_out[which] = jnp.broadcast_to(jnp.sum(pick * block, axis=1, keepdims=True), (CAP, LANES))
        if which == 0:
            pick = pick.astype(jnp.bfloat16)
            q_out[...] = jnp.dot(pick, q_ref[...], preferred_element_type=jnp.float32).astype(jnp.bfloat16)


def residual_kernel(Z, levels_ref, mask_ref, target_ref, res_ref, after_ref, res_out, target_out, chosen_out, weight_out):
    s, z, y, _, _, c = place()
    pick = jnp.where(slots_of(mask_ref[pl.ds(s, 1), :]), 1.0, 0.0)
    tok = pick.shape[1]
    chosen_out[...] = jnp.concatenate([pick, jnp.zeros((LANES - CAP, tok), jnp.float32)], axis=0)
    block = lax.shift_right_logical(lax.broadcasted_iota(jnp.int32, (8, tok), 1), SHIFT)
    weight = jnp.ones((8, tok), jnp.float32)
    for b in range(tok // BLOCK):
        weight = jnp.where(block == b, (levels_ref[s * (tok // BLOCK) + b] + 1).astype(jnp.float32), weight)
    weight_out[...] = weight
    pick = pick.astype(jnp.bfloat16)
    res_out[...] = jnp.dot(pick, res_ref[...], preferred_element_type=jnp.float32).astype(jnp.bfloat16)
    wide = target_out.shape[1]
    lane = lax.broadcasted_iota(jnp.int32, (8, wide), 1)
    found = jnp.zeros((8, wide), jnp.float32)
    for p, (k, other) in enumerate(row_order(Z)):
        src = swap_z(z, k, Z) * Y + (1 - y if other else y)
        hit = jnp.where(slots_of(mask_ref[pl.ds(src, 1), :]), 1.0, 0.0)
        half = jnp.where(c == 0, hit[:HALF], hit[HALF:])
        hit = jnp.concatenate([half, jnp.zeros((LANES - HALF, half.shape[1]), jnp.float32)], axis=0)
        row = jnp.broadcast_to(target_ref[pl.ds(src, 1), :].astype(jnp.float32), (8, target_ref.shape[1]))
        ids = exact_dot(row, hit, NT)
        ids = jnp.concatenate([ids] + [jnp.zeros((8, LANES), jnp.float32)] * (wide // LANES - 1), axis=1)
        ids = pltpu.roll(ids, p * HALF, 1) if p else ids
        found = jnp.where((lane >= p * HALF) & (lane < (p + 1) * HALF), ids, found)
    target_out[...] = found.astype(jnp.int32)


def stage_kernel(n, after, *refs):
    sems = refs[-1]
    copies = [pltpu.make_async_copy(refs[i], refs[n + i], sems.at[i]) for i in range(n)]
    for copy in copies:
        copy.start()
    for copy in copies:
        copy.wait()


def stage(after, *arrays):
    n = len(arrays)
    return call(
        functools.partial(stage_kernel, n),
        tuple(jax.ShapeDtypeStruct(a.shape, a.dtype) for a in arrays),
        (after, *arrays),
        1,
        scratch=[pltpu.SemaphoreType.DMA((n,))],
        specs=[ANY] * (n + 1),
        out_specs=(ANY,) * n,
    )


def split3(value):
    high = value.astype(jnp.bfloat16).astype(jnp.float32)
    rest = value - high
    mid = rest.astype(jnp.bfloat16).astype(jnp.float32)
    return high, mid, rest - mid


def attend_kernel(Z, heads, kv_heads, S, blk_ref, q_own, q_other, kn_ref, vn_ref, *refs):
    s, z, y, _, _, _ = place()
    *pieces, own_out, own_lse, other_out = refs
    passed = pieces.pop() if Z == 4 else None

    def piece(k, part, cols):
        block = pieces[k][part][:, cols]
        return block if passed is None or k != 2 else jnp.where(z == Z - 1, passed[part][:, cols], block)

    group = heads // kv_heads
    tok = kn_ref.shape[0]
    per_dev = tok // BLOCK
    scale = HEAD_DIM ** (-0.5)
    lane = lax.broadcasted_iota(jnp.int32, (CAP, LANES), 1)
    key_block = lax.shift_right_logical(lax.broadcasted_iota(jnp.int32, (CAP, tok), 1), SHIFT)
    for which in range(2):
        q_ref = (q_own, q_other)[which]
        slot_block = blk_ref[which][:, :1].astype(jnp.int32)
        row_block = slot_block + (s if which == 0 else s + 1 - 2 * y) * per_dev
        bias = []
        for k in range(Z):
            source = jnp.where(z >= k, s - k * Y, S)
            seen = (key_block + source * per_dev) < row_block
            bias.append(jnp.concatenate([jnp.where(seen, 0.0, very_low)] * group, axis=0))
        if which == 0:
            bias.append(jnp.concatenate([jnp.where(key_block == slot_block, 0.0, very_low)] * group, axis=0))
        lse_all = jnp.zeros((CAP, LANES), jnp.float32)
        for g in range(kv_heads):
            cols = slice(g * HEAD_DIM, (g + 1) * HEAD_DIM)
            q_g = jnp.concatenate(
                [q_ref[:, (g * group + h) * HEAD_DIM : (g * group + h + 1) * HEAD_DIM] for h in range(group)], axis=0
            )
            keys = [piece(k, 0, cols) for k in range(Z)]
            values = [piece(k, 1, cols) for k in range(Z)]
            if which == 0:
                keys.append(kn_ref[:, cols])
                values.append(vn_ref[:, cols])
            scores = [
                lax.dot_general(q_g, k, NT, preferred_element_type=jnp.float32) * scale + b for k, b in zip(keys, bias)
            ]
            top = jnp.max(functools.reduce(jnp.maximum, scores), axis=1, keepdims=True)
            weights = [jnp.exp(score - top) for score in scores]
            total = jnp.sum(functools.reduce(jnp.add, weights), axis=1, keepdims=True)
            mixed = functools.reduce(
                jnp.add,
                [jnp.dot(w.astype(jnp.bfloat16), v, preferred_element_type=jnp.float32) for w, v in zip(weights, values)],
            )
            mixed = mixed / total
            lse = top + jnp.log(total)
            for h in range(group):
                head = g * group + h
                rows = slice(h * CAP, (h + 1) * CAP)
                at = slice(head * HEAD_DIM, (head + 1) * HEAD_DIM)
                lse_all = jnp.where(lane == head, lse[rows], lse_all)
                if which == 0:
                    own_out[:, at] = mixed[rows]
                else:
                    other_out[:, at] = mixed[rows].astype(jnp.bfloat16)
        if which == 0:
            own_lse[...] = lse_all
        else:
            high, mid, low = split3(lse_all)
            packed = high + pltpu.roll(mid, 32, 1) + pltpu.roll(low, 64, 1)
            other_out[:, heads * HEAD_DIM :] = packed.astype(jnp.bfloat16)


def project_kernel(heads, own_ref, lse_ref, got_ref, w_ref, mine_out, theirs_out):
    _, _, _, _, _, c = place()
    packed = got_ref[:, heads * HEAD_DIM :].astype(jnp.float32)
    got_lse = packed + pltpu.roll(packed, LANES - 32, 1) + pltpu.roll(packed, LANES - 64, 1)
    own_lse = lse_ref[...]
    top = jnp.maximum(own_lse, got_lse)
    w_own, w_got = jnp.exp(own_lse - top), jnp.exp(got_lse - top)
    total = w_own + w_got
    w_own, w_got = w_own / total, w_got / total
    parts = []
    for h in range(heads):
        at = slice(h * HEAD_DIM, (h + 1) * HEAD_DIM)
        joined = own_ref[:, at] * w_own[:, h : h + 1] + got_ref[:, at].astype(jnp.float32) * w_got[:, h : h + 1]
        parts.append(joined.astype(jnp.bfloat16))
    attention = jnp.concatenate(parts, axis=1)
    first = c == 0
    width = w_ref.shape[1]
    step = min(1024, width)
    for j in range(0, width, step):
        out = jnp.dot(attention, w_ref[:, j : j + step], preferred_element_type=jnp.float32)
        upper, lower = out[:HALF], out[HALF:]
        mine_out[:, j : j + step] = jnp.where(first, upper, lower)
        theirs_out[:, j : j + step] = jnp.where(first, lower, upper).astype(jnp.bfloat16)


def norm_kernel(share, mine_ref, res_ref, gain_ref, *refs):
    _, _, _, _, x, c = place()
    *got, full_out, own_out, normed = refs
    res = res_ref[...].astype(jnp.float32)
    hidden = mine_ref[...]
    for ref in got:
        hidden = hidden + ref[...].astype(jnp.float32)
    hidden = jnp.where(c == 0, res[:HALF], res[HALF:]) + hidden
    squares = jnp.sum(hidden * hidden, axis=1, keepdims=True)
    normed[...] = hidden * lax.rsqrt(squares / D + norm_eps) * gain_ref[...]
    full_out[...] = normed[...].astype(jnp.bfloat16)
    own_out[...] = normed[:, pl.ds(pl.multiple_of(x * share, LANES), share)].astype(jnp.bfloat16)


def groups_of(Z):
    return GROUPS if Z == 4 else [range(1, Z)]


def pieces_of(group, mixed, X):
    return X if not mixed else 4 if group in STRAIGHT else 3


def row_order(Z):
    return [(0, False), (0, True)] + [(k, other) for group in groups_of(Z) for other in (False, True) for k in group]


def logits_kernel(mixed, X, Z, V, target_ref, *refs):
    s, z, y, v, x, c = place()
    share = refs[0].shape[1] // X
    n_rows = Y * Z * HALF
    sizes = [len(g) for g in groups_of(Z)]
    counts = [pieces_of(g, mixed, X) for g in groups_of(Z)]
    n_refs = 2 + sum(counts)
    (own, across, *pieces), (w_own, w_other, out_ref, *rows) = refs[:n_refs], refs[n_refs:]
    base = 2 * HALF
    for k in range(X):
        at = pl.multiple_of(lax.rem(x + (X - k), X) * share, LANES)
        rows[k][:HALF] = own[:, pl.ds(at, share)]
        rows[k][HALF:base] = across[:, pl.ds(at, share)]
    for i, size in enumerate(sizes):
        n = size * HALF
        mine = pieces[sum(counts[:i]) : sum(counts[: i + 1])]
        if mixed and counts[i] == 4:
            for ref, (at, block) in zip(mine, ((0, rows[0]), (0, rows[1]), (n, rows[0]), (n, rows[1]))):
                block[base + at : base + at + n] = ref[...]
        elif mixed:
            column, step1, step2 = mine
            near, far = rows
            near[base : base + n] = column[...]
            far[base + n : base + 2 * n] = step2[n:]

            @pl.when(c == 0)
            def _(base=base, n=n, step1=step1, step2=step2):
                near[base + n : base + 2 * n] = step2[:n]
                far[base : base + n] = step1[...]

            @pl.when(c != 0)
            def _(base=base, n=n, step1=step1, step2=step2):
                near[base + n : base + 2 * n] = step1[...]
                far[base : base + n] = step2[:n]
        else:
            for k in range(X):
                rows[k][base : base + Y * n] = mine[k][...]
        base += Y * n
    logits = []
    for w in (w_own, w_other):
        total = None
        for k in range(X):
            at = pl.multiple_of(lax.rem(x + (X - k), X) * share, LANES)
            part = lax.dot_general(w[:, pl.ds(at, share)], rows[k][...], NT, preferred_element_type=jnp.float32)
            total = part if total is None else total + part
        logits.append(total)
    vocab_rows = w_own.shape[0]
    starts = [(s * V + v) * vocab_rows, (s * V + v + 1 - 2 * c) * vocab_rows]
    top = jnp.maximum(jnp.max(logits[0], axis=0, keepdims=True), jnp.max(logits[1], axis=0, keepdims=True))
    summed = 0.0
    picked = 0.0
    wanted = target_ref[0:1, :n_rows]
    for start, lg in zip(starts, logits):
        ids = lax.broadcasted_iota(jnp.int32, lg.shape, 0)
        summed = summed + jnp.sum(jnp.exp(lg - top), axis=0, keepdims=True)
        picked = picked + jnp.sum(jnp.where(ids == wanted - start, lg, 0.0), axis=0, keepdims=True)
    lse = top + jnp.log(summed)
    wide = target_ref.shape[1]
    pad = [jnp.zeros((1, wide - n_rows), jnp.float32)] if wide > n_rows else []
    lse = jnp.broadcast_to(jnp.concatenate([lse, *pad], axis=1), (8, wide))
    picked = jnp.broadcast_to(jnp.concatenate([picked, *pad], axis=1), (8, wide))
    lane = lax.broadcasted_iota(jnp.int32, (8, LANES), 1)
    for p, (k, other) in enumerate(row_order(Z)):
        a = pltpu.roll(lse, (wide - p * HALF) % wide, 1)[:, :LANES]
        b = pltpu.roll(picked, (wide - p * HALF + HALF) % wide, 1)[:, :LANES]
        row = jnp.where(lane < HALF, a, b)[0:1]
        first = (swap_z(z, k, Z) * Y + (1 - y if other else y)) * V
        for i in range(V):
            out_ref[first + i] = row


def loss_kernel(chosen_ref, weight_ref, got_ref, out_ref):
    got = got_ref[...]
    core = lax.rem(lax.broadcasted_iota(jnp.int32, got.shape, 0), C)
    lane = lax.broadcasted_iota(jnp.int32, (8, LANES), 1)
    nll = jnp.zeros((8, LANES), jnp.float32)
    for half in range(C):
        here = core == half
        best = jnp.max(jnp.where(here, got, -jnp.inf), axis=0, keepdims=True)
        total = jnp.sum(jnp.where(here, jnp.exp(got - best), 0.0), axis=0, keepdims=True)
        picked = jnp.broadcast_to(jnp.sum(jnp.where(here, got, 0.0), axis=0, keepdims=True), (8, LANES))
        value = best + jnp.log(total) - pltpu.roll(picked, LANES - HALF, 1)
        value = pltpu.roll(value, half * HALF, 1) if half else value
        nll = jnp.where((lane >= half * HALF) & (lane < (half + 1) * HALF), value, nll)
    token_nll = exact_dot(nll, chosen_ref[...], (((1,), (0,)), ((), ())))
    out_ref[...] = (token_nll / weight_ref[...])[0:1]


def shards(
    q_noised,
    key_clean,
    value_clean,
    key_noised,
    value_noised,
    out_weight,
    residual,
    norm_gain,
    head_weight,
    targets,
    mask_flags,
    levels,
):
    tok_rows, q_width = q_noised.shape
    width = residual.shape[1]
    heads_local = q_width // HEAD_DIM
    kv_local = key_clean.shape[1] // HEAD_DIM
    vocab_rows = head_weight.shape[0]
    S = lax.axis_size("seq")
    V = lax.axis_size("vocab")
    X = V // C
    Z = S // Y
    share = width // X
    every = [(zi, yi, xi, ci) for zi in range(Z) for yi in range(Y) for xi in range(X) for ci in range(C)]

    def permute(block, to):
        def dev(zi, yi, xi, ci):
            return ((zi * Y + yi) * X + xi) * C + ci

        return lax.ppermute(block, ("seq", "vocab"), [(dev(*e), dev(*to(*e))) for e in every if to(*e)[0] < Z])

    def core_flip(block):
        return permute(block, lambda a, b, e, f: (a, b, e, 1 - f))

    def x_shift(block, k):
        return permute(block, lambda a, b, e, f: (a, b, (e + k) % X, f))

    def y_flip(block):
        return permute(block, lambda a, b, e, f: (a, 1 - b, e, f))

    def z_up(block, k):
        return permute(block, lambda a, b, e, f: (a + k, b, e, f))

    def along_z(block, pairs):
        return permute(block, lambda a, b, e, f: (dict(pairs).get(a, Z), b, e, f))

    def z_swap(block, k):
        paired = Z & (Z - 1) == 0
        return permute(block, lambda a, b, e, f: (a ^ k if paired else (a + k) % Z, b, e, f))

    def mixed_flip(block, x_core):
        return permute(block, lambda a, b, e, f: (a, b, 1 - e, f) if f == x_core else (a, 1 - b, e, f))

    def struct(*shape, dtype=jnp.bfloat16):
        return jax.ShapeDtypeStruct(shape, dtype)

    all_mask = mask_flags.reshape(S, tok_rows)
    own_kv = jnp.stack([key_clean, value_clean])
    next_kv = z_up(own_kv, 1)
    if Z == 4:
        far_kv = along_z(own_kv, ((0, 3),))
        second_kv = along_z(own_kv, ((0, 2),))
        passed_kv = along_z(next_kv, ((2, 3),))
        pieces = [own_kv, next_kv, second_kv, far_kv, passed_kv]
    else:
        pieces = [own_kv, next_kv] + [z_up(own_kv, k) for k in range(2, Z)]
    queries, slot_blocks = call(
        select_kernel, (struct(CAP, q_width), struct(2, CAP, LANES, dtype=jnp.float32)), (all_mask, q_noised), 8
    )
    other_queries = y_flip(queries)
    other_head = core_flip(head_weight)
    keys_here, values_here = stage(queries, key_noised, value_noised)
    own_sum, own_lse, other_sum = call(
        functools.partial(attend_kernel, Z, heads_local, kv_local, S),
        (
            struct(CAP, q_width, dtype=jnp.float32),
            struct(CAP, LANES, dtype=jnp.float32),
            struct(CAP, q_width + LANES),
        ),
        (slot_blocks, queries, other_queries, keys_here, values_here, *pieces),
        16,
    )
    got_sum = y_flip(other_sum)
    (staged_out,) = stage(other_sum, out_weight)
    mine, theirs = call(
        functools.partial(project_kernel, heads_local),
        (struct(HALF, width, dtype=jnp.float32), struct(HALF, width)),
        (own_sum, own_lse, got_sum, staged_out),
        16,
    )

    mine = mine + core_flip(theirs).astype(jnp.float32)
    sent = mine.astype(jnp.bfloat16)
    n_rows = Y * Z * HALF
    wide = -(-n_rows // LANES) * LANES
    residual_sel, row_targets, chosen, weight = call(
        functools.partial(residual_kernel, Z),
        (
            struct(CAP, width),
            struct(8, wide, dtype=jnp.int32),
            struct(LANES, tok_rows, dtype=jnp.float32),
            struct(8, tok_rows, dtype=jnp.float32),
        ),
        (levels, all_mask, targets.reshape(S, tok_rows), residual, theirs),
        8,
        specs=[SMEM] + [VMEM] * 4,
    )
    own_full, own = call(
        functools.partial(norm_kernel, share),
        (struct(HALF, width), struct(HALF, share)),
        (mine, residual_sel, norm_gain.reshape(1, width), *[x_shift(sent, k) for k in range(1, X)]),
        8,
        scratch=[pltpu.VMEM((HALF, width), jnp.float32)],
    )

    slabs = {}
    for k in range(1, Z):
        slabs[k] = z_swap(own, k)
    across = y_flip(own_full)
    mixed = X == Y
    rows = []
    for group in groups_of(Z):
        n = len(group) * HALF
        column = jnp.stack([slabs[k] for k in group])
        if mixed and group in STRAIGHT:
            over_x = x_shift(column, 1)
            over_y = y_flip(column)
            over_xy = permute(column, lambda a, b, e, f: (a, 1 - b, 1 - e, f))
            rows += [a.reshape(n, share) for a in (column, over_x, over_y, over_xy)]
        elif mixed:
            step1 = mixed_flip(column, 0)
            both = jnp.stack([column, step1])
            step2 = mixed_flip(both, 1)
            rows += [column.reshape(n, share), step1.reshape(n, share), step2.reshape(Y * n, share)]
        else:
            pair = jnp.stack([column, y_flip(column)])
            rows += [pair.reshape(Y * n, share)] + [x_shift(pair, k).reshape(Y * n, share) for k in range(1, X)]
    staged = stage(own, head_weight, other_head)
    send = call(
        functools.partial(logits_kernel, mixed, X, Z, V),
        struct(S * V, 1, LANES, dtype=jnp.float32),
        (row_targets, own_full, across, *rows, *staged),
        24,
        4 * n_rows * width * vocab_rows,
        [pltpu.VMEM((n_rows, share), jnp.bfloat16)] * X,
    ).reshape(S * V, LANES)
    got = lax.all_to_all(send, ("seq", "vocab"), 0, 0, tiled=True)
    loss = call(loss_kernel, struct(1, tok_rows, dtype=jnp.float32), (chosen, weight, got), 4)
    return loss.reshape(tok_rows)


def solution(mesh):
    in_specs = (
        P("seq", "vocab"),
        P("seq", "vocab"),
        P("seq", "vocab"),
        P("seq", "vocab"),
        P("seq", "vocab"),
        P("vocab", None),
        P("seq", None),
        P(),
        P(("seq", "vocab"), None),
        P(),
        P(),
        P(),
    )
    return jax.shard_map(shards, mesh=mesh, in_specs=in_specs, out_specs=P("seq"), check_vma=False)
```

```python
import functools

import jax
import jax.numpy as jnp
from jax import lax
from jax.experimental import pallas as pl
from jax.experimental.pallas import tpu as pltpu
from jax.sharding import PartitionSpec as P


D = 4096
HEAD_DIM = 128
BLOCK = 32
CAP = 48
HALF = CAP // 2
LANES = 128
SHIFT = BLOCK.bit_length() - 1
C = 2
Y = 2

very_low = -1e30
norm_eps = 1e-06

GROUPS = [[1], [3], [2]]

VMEM = pl.BlockSpec(memory_space=pltpu.VMEM)
SMEM = pl.BlockSpec(memory_space=pltpu.SMEM)
ANY = pl.BlockSpec(memory_space=pl.ANY)
NT = (((1,), (1,)), ((), ()))
MIB = 1 << 20


def call(kernel, outs, args, mib, flops=0, scratch=(), specs=None, out_specs=None):
    n_bytes = sum(a.size * a.dtype.itemsize for a in args)
    return pl.pallas_call(
        kernel,
        out_shape=outs,
        in_specs=specs or [VMEM] * len(args),
        out_specs=out_specs or jax.tree.map(lambda _: VMEM, outs),
        scratch_shapes=list(scratch),
        compiler_params=pltpu.CompilerParams(vmem_limit_bytes=mib * MIB),
        cost_estimate=pl.CostEstimate(flops=flops, bytes_accessed=n_bytes, transcendentals=0),
    )(*args)


def place():
    s, v = lax.axis_index("seq"), lax.axis_index("vocab")
    return s, lax.div(s, Y), lax.rem(s, Y), v, lax.div(v, C), lax.rem(v, C)


def swap_z(z, k, Z):
    return jnp.bitwise_xor(z, k) if Z & (Z - 1) == 0 else lax.rem(z + (Z - k), Z)


def slots_of(row):
    tok = row.shape[1]
    upto = lax.broadcasted_iota(jnp.int32, (tok, tok), 0) <= lax.broadcasted_iota(jnp.int32, (tok, tok), 1)
    row = row.astype(jnp.float32)
    count = jnp.dot(jnp.broadcast_to(row, (8, tok)), upto.astype(jnp.float32), preferred_element_type=jnp.float32)[0:1]
    slots = lax.broadcasted_iota(jnp.int32, (CAP, tok), 0).astype(jnp.float32)
    return ((count - 1.0) == slots) & (row == 1.0)


def exact_dot(a, b, dims):
    return lax.dot_general(a, b, dims, precision=lax.Precision.HIGHEST, preferred_element_type=jnp.float32)


def select_kernel(mask_ref, q_ref, q_out, blk_out):
    s, _, y, _, _, _ = place()
    tok = mask_ref.shape[1]
    block = lax.shift_right_logical(lax.broadcasted_iota(jnp.int32, (CAP, tok), 1), SHIFT).astype(jnp.float32)
    for which in range(2):
        pick = jnp.where(slots_of(mask_ref[pl.ds(s if which == 0 else s + 1 - 2 * y, 1), :]), 1.0, 0.0)
        blk_out[which] = jnp.broadcast_to(jnp.sum(pick * block, axis=1, keepdims=True), (CAP, LANES))
        if which == 0:
            pick = pick.astype(jnp.bfloat16)
            q_out[...] = jnp.dot(pick, q_ref[...], preferred_element_type=jnp.float32).astype(jnp.bfloat16)


def residual_kernel(Z, levels_ref, mask_ref, target_ref, res_ref, after_ref, res_out, target_out, chosen_out, weight_out):
    s, z, y, _, _, c = place()
    pick = jnp.where(slots_of(mask_ref[pl.ds(s, 1), :]), 1.0, 0.0)
    tok = pick.shape[1]
    chosen_out[...] = jnp.concatenate([pick, jnp.zeros((LANES - CAP, tok), jnp.float32)], axis=0)
    block = lax.shift_right_logical(lax.broadcasted_iota(jnp.int32, (8, tok), 1), SHIFT)
    weight = jnp.ones((8, tok), jnp.float32)
    for b in range(tok // BLOCK):
        weight = jnp.where(block == b, (levels_ref[s * (tok // BLOCK) + b] + 1).astype(jnp.float32), weight)
    weight_out[...] = weight
    pick = pick.astype(jnp.bfloat16)
    res_out[...] = jnp.dot(pick, res_ref[...], preferred_element_type=jnp.float32).astype(jnp.bfloat16)
    wide = target_out.shape[1]
    lane = lax.broadcasted_iota(jnp.int32, (8, wide), 1)
    found = jnp.zeros((8, wide), jnp.float32)
    for p, (k, other) in enumerate(row_order(Z)):
        src = swap_z(z, k, Z) * Y + (1 - y if other else y)
        hit = jnp.where(slots_of(mask_ref[pl.ds(src, 1), :]), 1.0, 0.0)
        half = jnp.where(c == 0, hit[:HALF], hit[HALF:])
        hit = jnp.concatenate([half, jnp.zeros((LANES - HALF, half.shape[1]), jnp.float32)], axis=0)
        row = jnp.broadcast_to(target_ref[pl.ds(src, 1), :].astype(jnp.float32), (8, target_ref.shape[1]))
        ids = exact_dot(row, hit, NT)
        ids = jnp.concatenate([ids] + [jnp.zeros((8, LANES), jnp.float32)] * (wide // LANES - 1), axis=1)
        ids = pltpu.roll(ids, p * HALF, 1) if p else ids
        found = jnp.where((lane >= p * HALF) & (lane < (p + 1) * HALF), ids, found)
    target_out[...] = found.astype(jnp.int32)


def stage_kernel(n, after, *refs):
    sems = refs[-1]
    copies = [pltpu.make_async_copy(refs[i], refs[n + i], sems.at[i]) for i in range(n)]
    for copy in copies:
        copy.start()
    for copy in copies:
        copy.wait()


def stage(after, *arrays):
    n = len(arrays)
    return call(
        functools.partial(stage_kernel, n),
        tuple(jax.ShapeDtypeStruct(a.shape, a.dtype) for a in arrays),
        (after, *arrays),
        1,
        scratch=[pltpu.SemaphoreType.DMA((n,))],
        specs=[ANY] * (n + 1),
        out_specs=(ANY,) * n,
    )


def split3(value):
    high = value.astype(jnp.bfloat16).astype(jnp.float32)
    rest = value - high
    mid = rest.astype(jnp.bfloat16).astype(jnp.float32)
    return high, mid, rest - mid


def attend_kernel(Z, heads, kv_heads, S, blk_ref, q_own, q_other, kn_ref, vn_ref, *refs):
    s, z, y, _, _, _ = place()
    *pieces, own_out, own_lse, other_out = refs
    passed = pieces.pop() if Z == 4 else None

    def piece(k, part, cols):
        block = pieces[k][part][:, cols]
        return block if passed is None or k != 2 else jnp.where(z == Z - 1, passed[part][:, cols], block)

    group = heads // kv_heads
    tok = kn_ref.shape[0]
    per_dev = tok // BLOCK
    scale = HEAD_DIM ** (-0.5)
    lane = lax.broadcasted_iota(jnp.int32, (CAP, LANES), 1)
    key_block = lax.shift_right_logical(lax.broadcasted_iota(jnp.int32, (CAP, tok), 1), SHIFT)
    for which in range(2):
        q_ref = (q_own, q_other)[which]
        slot_block = blk_ref[which][:, :1].astype(jnp.int32)
        row_block = slot_block + (s if which == 0 else s + 1 - 2 * y) * per_dev
        bias = []
        for k in range(Z):
            source = jnp.where(z >= k, s - k * Y, S)
            seen = (key_block + source * per_dev) < row_block
            bias.append(jnp.concatenate([jnp.where(seen, 0.0, very_low)] * group, axis=0))
        if which == 0:
            bias.append(jnp.concatenate([jnp.where(key_block == slot_block, 0.0, very_low)] * group, axis=0))
        lse_all = jnp.zeros((CAP, LANES), jnp.float32)
        for g in range(kv_heads):
            cols = slice(g * HEAD_DIM, (g + 1) * HEAD_DIM)
            q_g = jnp.concatenate(
                [q_ref[:, (g * group + h) * HEAD_DIM : (g * group + h + 1) * HEAD_DIM] for h in range(group)], axis=0
            )
            keys = [piece(k, 0, cols) for k in range(Z)]
            values = [piece(k, 1, cols) for k in range(Z)]
            if which == 0:
                keys.append(kn_ref[:, cols])
                values.append(vn_ref[:, cols])
            scores = [
                lax.dot_general(q_g, k, NT, preferred_element_type=jnp.float32) * scale + b for k, b in zip(keys, bias)
            ]
            top = jnp.max(functools.reduce(jnp.maximum, scores), axis=1, keepdims=True)
            weights = [jnp.exp(score - top) for score in scores]
            total = jnp.sum(functools.reduce(jnp.add, weights), axis=1, keepdims=True)
            mixed = functools.reduce(
                jnp.add,
                [jnp.dot(w.astype(jnp.bfloat16), v, preferred_element_type=jnp.float32) for w, v in zip(weights, values)],
            )
            mixed = mixed / total
            lse = top + jnp.log(total)
            for h in range(group):
                head = g * group + h
                rows = slice(h * CAP, (h + 1) * CAP)
                at = slice(head * HEAD_DIM, (head + 1) * HEAD_DIM)
                lse_all = jnp.where(lane == head, lse[rows], lse_all)
                if which == 0:
                    own_out[:, at] = mixed[rows]
                else:
                    other_out[:, at] = mixed[rows].astype(jnp.bfloat16)
        if which == 0:
            own_lse[...] = lse_all
        else:
            high, mid, low = split3(lse_all)
            packed = high + pltpu.roll(mid, 32, 1) + pltpu.roll(low, 64, 1)
            other_out[:, heads * HEAD_DIM :] = packed.astype(jnp.bfloat16)


def project_kernel(heads, own_ref, lse_ref, got_ref, w_ref, mine_out, theirs_out):
    _, _, _, _, _, c = place()
    packed = got_ref[:, heads * HEAD_DIM :].astype(jnp.float32)
    got_lse = packed + pltpu.roll(packed, LANES - 32, 1) + pltpu.roll(packed, LANES - 64, 1)
    own_lse = lse_ref[...]
    top = jnp.maximum(own_lse, got_lse)
    w_own, w_got = jnp.exp(own_lse - top), jnp.exp(got_lse - top)
    total = w_own + w_got
    w_own, w_got = w_own / total, w_got / total
    parts = []
    for h in range(heads):
        at = slice(h * HEAD_DIM, (h + 1) * HEAD_DIM)
        joined = own_ref[:, at] * w_own[:, h : h + 1] + got_ref[:, at].astype(jnp.float32) * w_got[:, h : h + 1]
        parts.append(joined.astype(jnp.bfloat16))
    attention = jnp.concatenate(parts, axis=1)
    first = c == 0
    width = w_ref.shape[1]
    step = min(1024, width)
    for j in range(0, width, step):
        out = jnp.dot(attention, w_ref[:, j : j + step], preferred_element_type=jnp.float32)
        upper, lower = out[:HALF], out[HALF:]
        mine_out[:, j : j + step] = jnp.where(first, upper, lower)
        theirs_out[:, j : j + step] = jnp.where(first, lower, upper).astype(jnp.bfloat16)


def norm_kernel(share, mine_ref, res_ref, gain_ref, *refs):
    _, _, _, _, x, c = place()
    *got, full_out, own_out, normed = refs
    res = res_ref[...].astype(jnp.float32)
    hidden = mine_ref[...]
    for ref in got:
        hidden = hidden + ref[...].astype(jnp.float32)
    hidden = jnp.where(c == 0, res[:HALF], res[HALF:]) + hidden
    squares = jnp.sum(hidden * hidden, axis=1, keepdims=True)
    normed[...] = hidden * lax.rsqrt(squares / D + norm_eps) * gain_ref[...]
    full_out[...] = normed[...].astype(jnp.bfloat16)
    own_out[...] = normed[:, pl.ds(pl.multiple_of(x * share, LANES), share)].astype(jnp.bfloat16)


def groups_of(Z):
    return GROUPS if Z == 4 else [range(1, Z)]


def row_order(Z):
    return [(0, False), (0, True)] + [(k, other) for group in groups_of(Z) for other in (False, True) for k in group]


def logits_kernel(mixed, X, Z, V, target_ref, *refs):
    s, z, y, v, x, c = place()
    share = refs[0].shape[1] // X
    n_rows = Y * Z * HALF
    sizes = [len(g) for g in groups_of(Z)]
    n_refs = 2 + (3 if mixed else X) * len(sizes)
    (own, across, *pieces), (w_own, w_other, out_ref, *rows) = refs[:n_refs], refs[n_refs:]
    base = 2 * HALF
    for k in range(X):
        at = pl.multiple_of(lax.rem(x + (X - k), X) * share, LANES)
        rows[k][:HALF] = own[:, pl.ds(at, share)]
        rows[k][HALF:base] = across[:, pl.ds(at, share)]
    for i, size in enumerate(sizes):
        n = size * HALF
        if mixed:
            column, step1, step2 = pieces[3 * i : 3 * i + 3]
            near, far = rows
            near[base : base + n] = column[...]
            far[base + n : base + 2 * n] = step2[n:]

            @pl.when(c != 0)
            def _(base=base, n=n, step1=step1, step2=step2):
                near[base + n : base + 2 * n] = step2[:n]
                far[base : base + n] = step1[...]

            @pl.when(c == 0)
            def _(base=base, n=n, step1=step1, step2=step2):
                near[base + n : base + 2 * n] = step1[...]
                far[base : base + n] = step2[:n]
        else:
            for k in range(X):
                rows[k][base : base + Y * n] = pieces[X * i + k][...]
        base += Y * n
    logits = []
    for w in (w_own, w_other):
        total = None
        for k in range(X):
            at = pl.multiple_of(lax.rem(x + (X - k), X) * share, LANES)
            part = lax.dot_general(w[:, pl.ds(at, share)], rows[k][...], NT, preferred_element_type=jnp.float32)
            total = part if total is None else total + part
        logits.append(total)
    vocab_rows = w_own.shape[0]
    starts = [(s * V + v) * vocab_rows, (s * V + v + 1 - 2 * c) * vocab_rows]
    top = jnp.maximum(jnp.max(logits[0], axis=0, keepdims=True), jnp.max(logits[1], axis=0, keepdims=True))
    summed = 0.0
    picked = 0.0
    wanted = target_ref[0:1, :n_rows]
    for start, lg in zip(starts, logits):
        ids = lax.broadcasted_iota(jnp.int32, lg.shape, 0)
        summed = summed + jnp.sum(jnp.exp(lg - top), axis=0, keepdims=True)
        picked = picked + jnp.sum(jnp.where(ids == wanted - start, lg, 0.0), axis=0, keepdims=True)
    lse = top + jnp.log(summed)
    wide = target_ref.shape[1]
    pad = [jnp.zeros((1, wide - n_rows), jnp.float32)] if wide > n_rows else []
    lse = jnp.broadcast_to(jnp.concatenate([lse, *pad], axis=1), (8, wide))
    picked = jnp.broadcast_to(jnp.concatenate([picked, *pad], axis=1), (8, wide))
    lane = lax.broadcasted_iota(jnp.int32, (8, LANES), 1)
    for p, (k, other) in enumerate(row_order(Z)):
        a = pltpu.roll(lse, (wide - p * HALF) % wide, 1)[:, :LANES]
        b = pltpu.roll(picked, (wide - p * HALF + HALF) % wide, 1)[:, :LANES]
        row = jnp.where(lane < HALF, a, b)[0:1]
        first = (swap_z(z, k, Z) * Y + (1 - y if other else y)) * V
        for i in range(V):
            out_ref[first + i] = row


def loss_kernel(chosen_ref, weight_ref, got_ref, out_ref):
    got = got_ref[...]
    core = lax.rem(lax.broadcasted_iota(jnp.int32, got.shape, 0), C)
    lane = lax.broadcasted_iota(jnp.int32, (8, LANES), 1)
    nll = jnp.zeros((8, LANES), jnp.float32)
    for half in range(C):
        here = core == half
        best = jnp.max(jnp.where(here, got, -jnp.inf), axis=0, keepdims=True)
        total = jnp.sum(jnp.where(here, jnp.exp(got - best), 0.0), axis=0, keepdims=True)
        picked = jnp.broadcast_to(jnp.sum(jnp.where(here, got, 0.0), axis=0, keepdims=True), (8, LANES))
        value = best + jnp.log(total) - pltpu.roll(picked, LANES - HALF, 1)
        value = pltpu.roll(value, half * HALF, 1) if half else value
        nll = jnp.where((lane >= half * HALF) & (lane < (half + 1) * HALF), value, nll)
    token_nll = exact_dot(nll, chosen_ref[...], (((1,), (0,)), ((), ())))
    out_ref[...] = (token_nll / weight_ref[...])[0:1]


def shards(
    q_noised,
    key_clean,
    value_clean,
    key_noised,
    value_noised,
    out_weight,
    residual,
    norm_gain,
    head_weight,
    targets,
    mask_flags,
    levels,
):
    tok_rows, q_width = q_noised.shape
    width = residual.shape[1]
    heads_local = q_width // HEAD_DIM
    kv_local = key_clean.shape[1] // HEAD_DIM
    vocab_rows = head_weight.shape[0]
    S = lax.axis_size("seq")
    V = lax.axis_size("vocab")
    X = V // C
    Z = S // Y
    share = width // X
    every = [(zi, yi, xi, ci) for zi in range(Z) for yi in range(Y) for xi in range(X) for ci in range(C)]

    def permute(block, to):
        def dev(zi, yi, xi, ci):
            return ((zi * Y + yi) * X + xi) * C + ci

        return lax.ppermute(block, ("seq", "vocab"), [(dev(*e), dev(*to(*e))) for e in every if to(*e)[0] < Z])

    def core_flip(block):
        return permute(block, lambda a, b, e, f: (a, b, e, 1 - f))

    def x_shift(block, k):
        return permute(block, lambda a, b, e, f: (a, b, (e + k) % X, f))

    def y_flip(block):
        return permute(block, lambda a, b, e, f: (a, 1 - b, e, f))

    def z_up(block, k):
        return permute(block, lambda a, b, e, f: (a + k, b, e, f))

    def along_z(block, pairs):
        return permute(block, lambda a, b, e, f: (dict(pairs).get(a, Z), b, e, f))

    def z_swap(block, k):
        paired = Z & (Z - 1) == 0
        return permute(block, lambda a, b, e, f: (a ^ k if paired else (a + k) % Z, b, e, f))

    def mixed_flip(block, x_core):
        return permute(block, lambda a, b, e, f: (a, b, 1 - e, f) if f == x_core else (a, 1 - b, e, f))

    def struct(*shape, dtype=jnp.bfloat16):
        return jax.ShapeDtypeStruct(shape, dtype)

    all_mask = mask_flags.reshape(S, tok_rows)
    own_kv = jnp.stack([key_clean, value_clean])
    next_kv = z_up(own_kv, 1)
    if Z == 4:
        far_kv = along_z(own_kv, ((0, 3),))
        second_kv = along_z(own_kv, ((0, 2),))
        passed_kv = along_z(next_kv, ((2, 3),))
        pieces = [own_kv, next_kv, second_kv, far_kv, passed_kv]
    else:
        pieces = [own_kv, next_kv] + [z_up(own_kv, k) for k in range(2, Z)]
    queries, slot_blocks = call(
        select_kernel, (struct(CAP, q_width), struct(2, CAP, LANES, dtype=jnp.float32)), (all_mask, q_noised), 8
    )
    other_queries = y_flip(queries)
    other_head = core_flip(head_weight)
    keys_here, values_here = stage(queries, key_noised, value_noised)
    own_sum, own_lse, other_sum = call(
        functools.partial(attend_kernel, Z, heads_local, kv_local, S),
        (
            struct(CAP, q_width, dtype=jnp.float32),
            struct(CAP, LANES, dtype=jnp.float32),
            struct(CAP, q_width + LANES),
        ),
        (slot_blocks, queries, other_queries, keys_here, values_here, *pieces),
        16,
    )
    got_sum = y_flip(other_sum)
    (staged_out,) = stage(other_sum, out_weight)
    mine, theirs = call(
        functools.partial(project_kernel, heads_local),
        (struct(HALF, width, dtype=jnp.float32), struct(HALF, width)),
        (own_sum, own_lse, got_sum, staged_out),
        16,
    )

    mine = mine + core_flip(theirs).astype(jnp.float32)
    sent = mine.astype(jnp.bfloat16)
    n_rows = Y * Z * HALF
    wide = -(-n_rows // LANES) * LANES
    residual_sel, row_targets, chosen, weight = call(
        functools.partial(residual_kernel, Z),
        (
            struct(CAP, width),
            struct(8, wide, dtype=jnp.int32),
            struct(LANES, tok_rows, dtype=jnp.float32),
            struct(8, tok_rows, dtype=jnp.float32),
        ),
        (levels, all_mask, targets.reshape(S, tok_rows), residual, theirs),
        8,
        specs=[SMEM] + [VMEM] * 4,
    )
    own_full, own = call(
        functools.partial(norm_kernel, share),
        (struct(HALF, width), struct(HALF, share)),
        (mine, residual_sel, norm_gain.reshape(1, width), *[x_shift(sent, k) for k in range(1, X)]),
        8,
        scratch=[pltpu.VMEM((HALF, width), jnp.float32)],
    )

    slabs = {}
    for k in range(1, Z):
        slabs[k] = z_swap(own, k)
    across = y_flip(own_full)
    mixed = X == Y
    rows = []
    for group in groups_of(Z):
        n = len(group) * HALF
        column = jnp.stack([slabs[k] for k in group])
        if mixed:
            step1 = mixed_flip(column, 1)
            both = jnp.stack([column, step1])
            step2 = mixed_flip(both, 0)
            rows += [column.reshape(n, share), step1.reshape(n, share), step2.reshape(Y * n, share)]
        else:
            pair = jnp.stack([column, y_flip(column)])
            rows += [pair.reshape(Y * n, share)] + [x_shift(pair, k).reshape(Y * n, share) for k in range(1, X)]
    staged = stage(own, head_weight, other_head)
    send = call(
        functools.partial(logits_kernel, mixed, X, Z, V),
        struct(S * V, 1, LANES, dtype=jnp.float32),
        (row_targets, own_full, across, *rows, *staged),
        24,
        4 * n_rows * width * vocab_rows,
        [pltpu.VMEM((n_rows, share), jnp.bfloat16)] * X,
    ).reshape(S * V, LANES)
    got = lax.all_to_all(send, ("seq", "vocab"), 0, 0, tiled=True)
    loss = call(loss_kernel, struct(1, tok_rows, dtype=jnp.float32), (chosen, weight, got), 4)
    return loss.reshape(tok_rows)


def solution(mesh):
    in_specs = (
        P("seq", "vocab"),
        P("seq", "vocab"),
        P("seq", "vocab"),
        P("seq", "vocab"),
        P("seq", "vocab"),
        P("vocab", None),
        P("seq", None),
        P(),
        P(("seq", "vocab"), None),
        P(),
        P(),
        P(),
    )
    return jax.shard_map(shards, mesh=mesh, in_specs=in_specs, out_specs=P("seq"), check_vma=False)
```
